256 devices in a mesh: pb: 8 (over x, y_hi), ka: 32 (over y_lo, z, core).
Axes of the slice: x: 4, y: 4 (y_hi: 2, y_lo: 2; y = y_hi * 2 + y_lo), z: 8, core: 2. Of those that a mesh axis runs over, the one named last changes fastest.
Arguments:
- queries: bfloat16 [32768, 2048], P(('pb', 'ka')), may hold values from -3 to 3
- keys: bfloat16 [32768, 2048], P(('pb', 'ka')), may hold values from -3 to 3
- values: bfloat16 [32768, 2048], P(('pb', 'ka')), may hold values from -3 to 3
- outputs: bfloat16 [32768, 2048], P(('pb', 'ka')), may hold values from -3 to 3
- d_out: bfloat16 [32768, 2048], P(('pb', 'ka')), may hold values from -16 to 16
- row_lse: float32 [16, 32768], P(None, ('pb', 'ka')), may hold values from 6.5 to 8.5
- adjacency: int32 [256, 2, 4, 1], P(('pb', 'ka')), may hold values from 0 to 1, as said below
Outputs:
- grad_queries: bfloat16 [32768, 2048], P(('pb', 'ka'))
- grad_keys: bfloat16 [32768, 2048], P(('pb', 'ka'))
- grad_values: bfloat16 [32768, 2048], P(('pb', 'ka'))
The draws below stay inside these ranges and needn't reach their ends.
Inputs may be any that keep to these rules, and one draw needn't show every extreme that they name: 1 where the query block attends that key block of its window, else 0; every query block attends its own key block, adjacency[b, 0, 0, 0] = 1.
All inputs are finite; a program needn't handle non-finite values.
Results may differ from the reference program's by a relative error of at most 0.0075.
Values may be sent and summed in bfloat16 or wider, within the bound.
No kernel may reach another device: no remote copies, remote signals or barrier semaphores. Data moves between devices by JAX's collectives and lax.ppermute only.
A program may use at most 128 MiB of HBM per device.

```python
import math
import jax
import jax.numpy as jnp
from jax import lax

HEADS = 16
HEAD_DIM = 128
BLOCK = 128
WINDOW = 4
TOK_DEV = 128
D = 2048
BLOCKS_DEV = 1
GRID_ROWS = 8
GRID_COLS = 32
TOKENS = 32768
QBLOCKS = 256


def draw_adjacency(key, part):
    level_key = jax.random.fold_in(key, 11)
    entry_key = jax.random.fold_in(key, 23)
    device_total = GRID_ROWS * GRID_COLS
    levels = jax.random.randint(level_key, (device_total,), 0, 4)
    shift_amount = jnp.where(levels == 0, 0, levels + 1).astype(jnp.int32)
    limits = jnp.right_shift(jnp.full((device_total,), 16, jnp.int32), shift_amount)
    per_block = jnp.repeat(limits, BLOCKS_DEV, total_repeat_length=QBLOCKS)
    rolls = jax.random.randint(entry_key, (QBLOCKS, 2, WINDOW, BLOCKS_DEV), 0, 16)
    present = rolls < per_block[:, None, None, None]
    block_ids = jnp.arange(QBLOCKS, dtype=jnp.int32) % BLOCKS_DEV
    row_ids = jnp.arange(2, dtype=jnp.int32)
    col_ids = jnp.arange(WINDOW, dtype=jnp.int32)
    key_ids = jnp.arange(BLOCKS_DEV, dtype=jnp.int32)
    own_block = (row_ids[None, :, None, None] == 0) & (col_ids[None, None, :, None] == 0) & (key_ids[None, None, None, :] == block_ids[:, None, None, None])
    return (present | own_block).astype(jnp.int32)


def shard_levels(key, extent, pieces, least, largest):
    loudness, own = 1.0, jax.random.fold_in(key, 6)
    for position, shards_of in pieces:
        draws = jnp.exp(jax.random.uniform(jax.random.fold_in(own, position), (shards_of,), jnp.float32, least / len(pieces), largest / len(pieces)))
        loudness = loudness * jnp.repeat(draws, extent[position] // shards_of).reshape([-1 if axis == position else 1 for axis in range(len(extent))])
    return loudness


def gaussian(key, shape, scale, limit, cuts=(), kind=jnp.bfloat16):
    drawn = jax.random.normal(key, shape, jnp.float32) * scale
    if len(cuts) > 0:
        drawn = shard_levels(key, shape, cuts, -0.22, 0.18) * drawn
    return jnp.clip(drawn, min=-limit, max=limit).astype(kind)


def setup_inputs(seed: int = 0) -> dict:
    seeds = jax.random.split(jax.random.key(seed), 8)
    queries = gaussian(seeds[0], (TOKENS, D), 1.0, 3.0, ((0, 256),))
    keys = gaussian(seeds[1], (TOKENS, D), 1.0, 3.0, ((0, 256),))
    values = gaussian(seeds[2], (TOKENS, D), 1.0, 3.0, ((0, 256),))
    outputs = gaussian(seeds[3], (TOKENS, D), 1.0, 3.0, ((0, 256),))
    d_out = gaussian(seeds[4], (TOKENS, D), 6.0, 16.0, ((0, 256),))
    row_lse = jnp.clip(6.5 + 2.0 * jax.random.uniform(seeds[5], (HEADS, TOKENS), jnp.float32) ** shard_levels(seeds[5], (HEADS, TOKENS), ((1, 256),), -0.2, 0.2), 6.5, 8.5)
    adjacency = draw_adjacency(jax.random.fold_in(seeds[7], 71), 0)
    return dict(queries=queries, keys=keys, values=values, outputs=outputs, d_out=d_out, row_lse=row_lse, adjacency=adjacency)


def spread_mask(block_mask):
    block_count = block_mask.shape[0]
    full = jnp.broadcast_to(block_mask[:, None, :, None], (block_count, BLOCK, block_count, BLOCK))
    return full.reshape(block_count * BLOCK, block_count * BLOCK)

def pair_terms(query_rows, grad_rows, row_norms, row_delta, key_rows, value_rows, allowed):
    inverse = 1.0 / math.sqrt(HEAD_DIM)
    query_heads = query_rows.astype(jnp.float32).reshape(TOK_DEV, HEADS, HEAD_DIM)
    grad_heads = grad_rows.astype(jnp.float32).reshape(TOK_DEV, HEADS, HEAD_DIM)
    key_heads = key_rows.astype(jnp.float32).reshape(TOK_DEV, HEADS, HEAD_DIM)
    value_heads = value_rows.astype(jnp.float32).reshape(TOK_DEV, HEADS, HEAD_DIM)
    scores = jnp.einsum('ihe,the->hit', query_heads, key_heads) * inverse
    prob_full = jnp.where(allowed[None], jnp.exp(scores - row_norms[:, :, None]), jnp.float32(0.0))
    prob_low = lax.optimization_barrier(prob_full.astype(jnp.bfloat16)).astype(jnp.float32)
    prob_grad = jnp.einsum('ihe,the->hit', grad_heads, value_heads)
    score_grad = (prob_full * (prob_grad - row_delta[:, :, None]) * inverse).astype(jnp.bfloat16)
    score_grad = lax.optimization_barrier(score_grad).astype(jnp.float32)
    grad_v = jnp.einsum('hit,ihe->the', prob_low, grad_heads).reshape(TOK_DEV, D)
    grad_q = jnp.einsum('hit,the->ihe', score_grad, key_heads).reshape(TOK_DEV, D)
    grad_k = jnp.einsum('hit,ihe->the', score_grad, query_heads).reshape(TOK_DEV, D)
    return (grad_q, grad_k, grad_v)

def add_rows(total, start, term):
    current = lax.dynamic_slice_in_dim(total, start, TOK_DEV, 0)
    return lax.dynamic_update_slice_in_dim(total, current + term, start, 0)

def reference(queries, keys, values, outputs, d_out, row_lse, adjacency):
    product = d_out.astype(jnp.float32) * outputs.astype(jnp.float32)
    delta_all = lax.optimization_barrier(jnp.sum(product.reshape(TOKENS, HEADS, HEAD_DIM), axis=2)).T

    def per_device(totals, device_index):
        grad_keys, grad_values = totals
        grid_row = device_index // GRID_COLS
        grid_col = device_index % GRID_COLS
        start = (device_index * TOK_DEV).astype(jnp.int32)
        query_rows = lax.dynamic_slice_in_dim(queries, start, TOK_DEV, 0)
        grad_rows = lax.dynamic_slice_in_dim(d_out, start, TOK_DEV, 0)
        row_norms = lax.dynamic_slice_in_dim(row_lse, start, TOK_DEV, 1)
        row_delta = lax.dynamic_slice_in_dim(delta_all, start, TOK_DEV, 1)
        blocks = lax.dynamic_slice_in_dim(adjacency, (device_index * BLOCKS_DEV).astype(jnp.int32), BLOCKS_DEV, 0)
        grad_query = jnp.zeros((TOK_DEV, D), jnp.float32)
        for row_step in range(2):
            for col_step in range(WINDOW):
                key_device = (grid_row + row_step) % GRID_ROWS * GRID_COLS + (grid_col + col_step) % GRID_COLS
                key_start = (key_device * TOK_DEV).astype(jnp.int32)
                key_rows = lax.dynamic_slice_in_dim(keys, key_start, TOK_DEV, 0)
                value_rows = lax.dynamic_slice_in_dim(values, key_start, TOK_DEV, 0)
                allowed = spread_mask(blocks[:, row_step, col_step, :] == 1)
                term_q, term_k, term_v = pair_terms(query_rows, grad_rows, row_norms, row_delta, key_rows, value_rows, allowed)
                grad_query = grad_query + term_q
                grad_keys = add_rows(grad_keys, key_start, term_k)
                grad_values = add_rows(grad_values, key_start, term_v)
        return ((grad_keys, grad_values), grad_query.astype(jnp.bfloat16))
    empty_rows = jnp.zeros((TOKENS, D), jnp.float32)
    device_list = jnp.arange(GRID_ROWS * GRID_COLS, dtype=jnp.int32)
    (grad_keys, grad_values), grad_blocks = lax.scan(per_device, (empty_rows, empty_rows), device_list)
    grad_queries = grad_blocks.reshape(TOKENS, D)
    return (grad_queries, grad_keys.astype(jnp.bfloat16), grad_values.astype(jnp.bfloat16))
```

```python
import functools
import math

import jax
import jax.numpy as jnp
from jax import lax
from jax.experimental import pallas as pl
from jax.experimental.pallas import tpu as pltpu
from jax.sharding import PartitionSpec as P

HEAD_DIM = 128
BLOCK = 128
WINDOW = 4
STAT = 16
HALF = 8
QROWS = 2 * BLOCK + STAT
KROWS = 2 * BLOCK
LOG2E = math.log2(math.e)
SCALE = 1.0 / math.sqrt(HEAD_DIM)
FAR_AWAY = 1e30
F32 = jnp.float32
BF16 = jnp.bfloat16


def three_pieces(value):
    high = value.astype(BF16).astype(F32)
    rest = value - high
    middle = rest.astype(BF16).astype(F32)
    return high, middle, rest - middle


def pack_head(adj_ref, q, g, o, lse_row):
    product = g.astype(F32) * o.astype(F32)
    delta_row = jnp.sum(product.T, axis=0, keepdims=True)
    rows = list(three_pieces(lse_row)) + list(three_pieces(delta_row))
    line = lax.broadcasted_iota(jnp.int32, (STAT, BLOCK), 0)
    stat = jnp.zeros((STAT, BLOCK), F32)
    for i, row in enumerate(rows):
        stat = jnp.where(line == i, jnp.broadcast_to(row, (STAT, BLOCK)), stat)
    for i in range(2 * WINDOW):
        flag = (adj_ref[i] == 1).astype(jnp.int32).astype(F32)
        stat = jnp.where(line == 8 + i, flag, stat)
    return stat.astype(BF16)


def pack_kernel(odd_ref, adj_ref, qa, ka, va, oa, ga, la, qb, kb, vb, ob, gb, lb,
                xqa, xka, xqb, xkb, near):
    heads = xqa.shape[0]
    for h in range(heads):
        cols = slice(h * HEAD_DIM, (h + 1) * HEAD_DIM)
        xqa[h, 0:128, :] = qa[:, cols]
        xqa[h, 128:256, :] = ga[:, cols]
        xqa[h, 256:272, :] = pack_head(adj_ref, qa[:, cols], ga[:, cols], oa[:, cols], la[h])
        xqb[h, 0:128, :] = qb[:, cols]
        xqb[h, 128:256, :] = gb[:, cols]
        xqb[h, 256:272, :] = pack_head(adj_ref, qb[:, cols], gb[:, cols], ob[:, cols], lb[h])
        xka[h, 0:128, :] = ka[:, cols]
        xka[h, 128:256, :] = va[:, cols]
        xkb[h, 0:128, :] = kb[:, cols]
        xkb[h, 128:256, :] = vb[:, cols]

    @pl.when(odd_ref[0] == 0)
    def _():
        near[...] = xqa[...]

    @pl.when(odd_ref[0] == 1)
    def _():
        near[:, 0:KROWS, :] = xkb[...]
        near[:, KROWS:QROWS, :] = jnp.zeros((heads, STAT, HEAD_DIM), BF16)


def pack(odd, adjacency, queries, keys, values, outputs, d_out, row_lse):
    step = 2
    grid = (HALF // step,)
    lse3 = row_lse.reshape(2 * HALF, 1, BLOCK)

    def rows(shift):
        return pl.BlockSpec((BLOCK, step * HEAD_DIM), lambda i: (0, i + shift))

    def lse(shift):
        return pl.BlockSpec((step, 1, BLOCK), lambda i: (i + shift, 0, 0))

    def out(count):
        return pl.BlockSpec((step, count, HEAD_DIM), lambda i: (i, 0, 0))

    far = HALF // step
    smem = pl.BlockSpec(memory_space=pltpu.SMEM)
    shapes = [QROWS, KROWS, QROWS, KROWS, QROWS]
    return pl.pallas_call(
        pack_kernel,
        grid=grid,
        in_specs=[smem, smem] + [rows(0)] * 5 + [lse(0)] + [rows(far)] * 5 + [lse(far)],
        out_specs=[out(s) for s in shapes],
        out_shape=[jax.ShapeDtypeStruct((HALF, s, HEAD_DIM), BF16) for s in shapes],
        cost_estimate=pl.CostEstimate(flops=10**6, bytes_accessed=5 * 2**20, transcendentals=0),
        name="pack",
    )(odd, adjacency, queries, keys, values, outputs, d_out, lse3,
      queries, keys, values, outputs, d_out, lse3)


def contract(a, b, da, db):
    return lax.dot_general(a, b, (((da,), (db,)), ((), ())), preferred_element_type=F32)


def unpack_stat(stat, row, slot_flag):
    stat = stat.astype(F32)
    lse = stat[0:1] + stat[1:2] + stat[2:3]
    delta = stat[3:4] + stat[4:5] + stat[5:6]
    keep = slot_flag(stat, 8 + WINDOW * row) > 0.5
    return jnp.where(keep, lse * LOG2E, FAR_AWAY), delta


def flag_of(w):
    return lambda stat, base: stat[base + w:base + w + 1]


def flag_by_parity(odd, w_even, w_odd):
    return lambda stat, base: jnp.where(
        odd == 1, stat[base + w_odd:base + w_odd + 1], stat[base + w_even:base + w_even + 1])


def terms(q, g, k, v, lse, delta):
    scores = contract(k, q, 1, 1) * (SCALE * LOG2E)
    prob = jnp.exp2(scores - lse)
    grad = prob * (contract(v, g, 1, 1) - delta)
    low = prob.astype(BF16)
    grad = grad.astype(BF16)
    dv = contract(low, g, 1, 0)
    dk = contract(grad, q, 1, 0) * SCALE
    dq = contract(grad, k, 0, 0) * SCALE
    return dq, dk, dv


def attend_kernel(odd_ref, xqa, near, q2, q3, q1, xka, fk, xqb, fq, xkb, k2, k3, k1,
                  q_own, q_two, k_own, k_two, kv_a, q_b, swap_out, down_out, up_out, far_k_out, far_q_out):
    odd = odd_ref[0]
    is_odd = odd == 1

    one = jnp.where(is_odd, near[0], q1[0])
    slots = [xqa[0], one, q2[0], q3[0]]
    q = jnp.concatenate([s[0:128] for s in slots], axis=0)
    g = jnp.concatenate([s[128:256] for s in slots], axis=0)
    flags = [flag_of(0), flag_by_parity(odd, 3, 1), flag_of(2), flag_by_parity(odd, 1, 3)]
    lse, delta = [], []
    for row in range(2):
        both = [unpack_stat(s[256:272], row, f) for s, f in zip(slots, flags)]
        lse.append(jnp.broadcast_to(jnp.concatenate([b[0] for b in both], axis=1), (128, 512)))
        delta = jnp.concatenate([b[1] for b in both], axis=1)
    k = jnp.concatenate([xka[0, 0:128], fk[0, 0:128]], axis=0)
    v = jnp.concatenate([xka[0, 128:256], fk[0, 128:256]], axis=0)
    dq, dk, dv = terms(q, g, k, v, jnp.concatenate(lse, axis=0), delta)
    q_own[0] = dq[0:128]
    down_out[0] = dq[128:256].astype(BF16)
    q_two[0] = dq[256:384]
    swap_out[0, 0:128] = dq[384:512].astype(BF16)
    kv_a[0, 0:128] = dk[0:128]
    kv_a[0, 128:256] = dv[0:128]
    far_k_out[0, 0:128] = dk[128:256].astype(BF16)
    far_k_out[0, 128:256] = dv[128:256].astype(BF16)

    one = jnp.where(is_odd, k1[0], near_k(near))
    slots = [xkb[0], one, k2[0], k3[0]]
    k = jnp.concatenate([s[0:128] for s in slots], axis=0)
    v = jnp.concatenate([s[128:256] for s in slots], axis=0)
    q = jnp.concatenate([xqb[0, 0:128], fq[0, 0:128]], axis=0)
    g = jnp.concatenate([xqb[0, 128:256], fq[0, 128:256]], axis=0)
    flags = [flag_of(0), flag_by_parity(odd, 1, 3), flag_of(2), flag_by_parity(odd, 3, 1)]
    stat_own, stat_far = xqb[0, 256:272], fq[0, 256:272]
    lse = []
    for f in flags:
        own, own_delta = unpack_stat(stat_own, 0, f)
        far, far_delta = unpack_stat(stat_far, 1, f)
        lse.append(jnp.broadcast_to(jnp.concatenate([own, far], axis=1), (128, 256)))
        delta = jnp.concatenate([own_delta, far_delta], axis=1)
    dq, dk, dv = terms(q, g, k, v, jnp.concatenate(lse, axis=0), delta)
    q_b[0] = dq[0:128]
    far_q_out[0] = dq[128:256].astype(BF16)
    k_own[0, 0:128] = dk[0:128]
    k_own[0, 128:256] = dv[0:128]
    up_out[0, 0:128] = dk[128:256].astype(BF16)
    up_out[0, 128:256] = dv[128:256].astype(BF16)
    k_two[0, 0:128] = dk[256:384]
    k_two[0, 128:256] = dv[256:384]
    swap_out[0, 128:256] = dk[384:512].astype(BF16)
    swap_out[0, 256:384] = dv[384:512].astype(BF16)


def near_k(near):
    return near[0, 0:KROWS]


def per_head(count):
    return pl.BlockSpec((1, count, HEAD_DIM), lambda i: (i, 0, 0))


def attend(odd, xqa, near, q2, q3, q1, xka, fk, xqb, fq, xkb, k2, k3, k1):
    in_rows = [QROWS] * 5 + [KROWS] * 2 + [QROWS] * 2 + [KROWS] * 4
    outs = [(128, F32), (128, F32), (256, F32), (256, F32), (256, F32), (128, F32),
            (384, BF16), (128, BF16), (256, BF16), (256, BF16), (128, BF16)]
    return pl.pallas_call(
        attend_kernel,
        grid=(HALF,),
        in_specs=[pl.BlockSpec(memory_space=pltpu.SMEM)] + [per_head(r) for r in in_rows],
        out_specs=[per_head(r) for r, _ in outs],
        out_shape=[jax.ShapeDtypeStruct((HALF, r, HEAD_DIM), t) for r, t in outs],
        cost_estimate=pl.CostEstimate(flops=27 * 10**8, bytes_accessed=14 * 2**20, transcendentals=2**21),
        name="attend",
    )(odd, xqa, near, q2, q3, q1, xka, fk, xqb, fq, xkb, k2, k3, k1)


def combine_kernel(odd_ref, q_two, k_two, swapped, down, up, down_sum, up_sum):
    odd = odd_ref[0]
    from_down = jnp.where(odd == 1, down[...].astype(F32), 0.0)
    from_up = jnp.where(odd == 1, 0.0, up[...].astype(F32))
    down_sum[...] = (q_two[...] + swapped[:, 0:128].astype(F32) + from_down).astype(BF16)
    up_sum[...] = (k_two[...] + swapped[:, 128:384].astype(F32) + from_up).astype(BF16)


def heads_block(step, count):
    return pl.BlockSpec((step, count, HEAD_DIM), lambda i: (i, 0, 0))


def combine(odd, q_two, k_two, swapped, down, up):
    step = 2
    return pl.pallas_call(
        combine_kernel,
        grid=(HALF // step,),
        in_specs=[pl.BlockSpec(memory_space=pltpu.SMEM)]
        + [heads_block(step, r) for r in (128, 256, 384, 128, 256)],
        out_specs=[heads_block(step, 128), heads_block(step, 256)],
        out_shape=[jax.ShapeDtypeStruct((HALF, r, HEAD_DIM), BF16) for r in (128, 256)],
        cost_estimate=pl.CostEstimate(flops=10**6, bytes_accessed=4 * 2**20, transcendentals=0),
        name="combine",
    )(odd, q_two, k_two, swapped, down, up)


def finish_kernel(odd_ref, q_own, k_own, kv_a, q_b, down, up, down_sum, up_sum, far_k, far_q,
                  dq_a, dk_a, dv_a, dq_b, dk_b, dv_b):
    odd = odd_ref[0]
    for h in range(q_own.shape[0]):
        cols = slice(h * HEAD_DIM, (h + 1) * HEAD_DIM)
        from_down = jnp.where(odd == 1, 0.0, down[h].astype(F32))
        from_up = jnp.where(odd == 1, up[h].astype(F32), 0.0)
        dq_a[:, cols] = (q_own[h] + down_sum[h].astype(F32) + from_down).astype(BF16)
        total = kv_a[h] + far_k[h].astype(F32)
        dk_a[:, cols] = total[0:128].astype(BF16)
        dv_a[:, cols] = total[128:256].astype(BF16)
        dq_b[:, cols] = (q_b[h] + far_q[h].astype(F32)).astype(BF16)
        total = k_own[h] + up_sum[h].astype(F32) + from_up
        dk_b[:, cols] = total[0:128].astype(BF16)
        dv_b[:, cols] = total[128:256].astype(BF16)


def finish(odd, q_own, k_own, kv_a, q_b, down, up, down_sum, up_sum, far_k, far_q):
    step = 2
    width = step * HEAD_DIM
    column = pl.BlockSpec((BLOCK, width), lambda i: (0, i))
    parts = pl.pallas_call(
        finish_kernel,
        grid=(HALF // step,),
        in_specs=[pl.BlockSpec(memory_space=pltpu.SMEM)]
        + [heads_block(step, r) for r in (128, 256, 256, 128, 128, 256, 128, 256, 256, 128)],
        out_specs=[column] * 6,
        out_shape=[jax.ShapeDtypeStruct((BLOCK, HALF * HEAD_DIM), BF16)] * 6,
        cost_estimate=pl.CostEstimate(flops=10**6, bytes_accessed=6 * 2**20, transcendentals=0),
        name="finish",
    )(odd, q_own, k_own, kv_a, q_b, down, up, down_sum, up_sum, far_k, far_q)
    return [jnp.concatenate([parts[i], parts[i + 3]], axis=1) for i in range(3)]


def moved(value, axis, steps):
    count = lax.axis_size(axis)
    return lax.ppermute(value, axis, [(i, (i + steps) % count) for i in range(count)])


def exchanged(value):
    count = lax.axis_size("ka")
    return lax.ppermute(value, "ka", [(i, i ^ 1) for i in range(count)])


def relayed(value, first, steps):
    count = lax.axis_size("ka")
    return lax.ppermute(value, "ka", [(i, (i + steps) % count) for i in range(first, count, 2)])


def local(queries, keys, values, outputs, d_out, row_lse, adjacency):
    odd = (lax.axis_index("ka") % 2).astype(jnp.int32).reshape(1)
    flags = adjacency.reshape(2 * WINDOW)
    xqa, xka, xqb, xkb, near = pack(odd, flags, queries, keys, values, outputs, d_out, row_lse)
    q2 = moved(xqa, "ka", 2)
    k2 = moved(xkb, "ka", -2)
    near = exchanged(near)
    fk = moved(xka, "pb", -1)
    fq = moved(xqb, "pb", 1)
    q1 = relayed(q2, 1, 1)
    k1 = relayed(k2, 0, -1)
    q3 = exchanged(q2)
    k3 = exchanged(k2)
    (q_own, q_two, k_own, k_two, kv_a, q_b, swap_out, down_out, up_out, far_k, far_q) = attend(
        odd, xqa, near, q2, q3, q1, xka, fk, xqb, fq, xkb, k2, k3, k1)
    down = moved(down_out, "ka", -1)
    up = moved(up_out, "ka", 1)
    swapped = exchanged(swap_out)
    far_k = moved(far_k, "pb", 1)
    far_q = moved(far_q, "pb", -1)
    down_sum, up_sum = combine(odd, q_two, k_two, swapped, down, up)
    down_sum = moved(down_sum, "ka", -2)
    up_sum = moved(up_sum, "ka", 2)
    dq, dk, dv = finish(odd, q_own, k_own, kv_a, q_b, down, up, down_sum, up_sum, far_k, far_q)
    return dq, dk, dv


def solution(mesh):
    rows = P(("pb", "ka"), None)
    placed = (rows, rows, rows, rows, rows, P(None, ("pb", "ka")), P(("pb", "ka"), None, None, None))
    return jax.shard_map(
        local,
        mesh=mesh,
        in_specs=placed,
        out_specs=(rows, rows, rows),
        check_vma=False,
    )
```

```python
import functools
import math

import jax
import jax.numpy as jnp
from jax import lax
from jax.experimental import pallas as pl
from jax.experimental.pallas import tpu as pltpu
from jax.sharding import PartitionSpec as P

HEAD_DIM = 128
BLOCK = 128
WINDOW = 4
STAT = 16
HALF = 8
QROWS = 2 * BLOCK + STAT
KROWS = 2 * BLOCK
LOG2E = math.log2(math.e)
SCALE = 1.0 / math.sqrt(HEAD_DIM)
FAR_AWAY = 1e30
F32 = jnp.float32
BF16 = jnp.bfloat16


def three_pieces(value):
    high = value.astype(BF16).astype(F32)
    rest = value - high
    middle = rest.astype(BF16).astype(F32)
    return high, middle, rest - middle


def pack_head(adj_ref, g, o, lse_row):
    down = lax.broadcasted_iota(jnp.int32, (BLOCK, BLOCK), 0)
    across = lax.broadcasted_iota(jnp.int32, (BLOCK, BLOCK), 1)
    product = contract(o, g, 1, 1)
    delta_row = jnp.sum(jnp.where(down == across, product, 0.0), axis=0, keepdims=True)
    rows = list(three_pieces(lse_row)) + list(three_pieces(delta_row))
    line = lax.broadcasted_iota(jnp.int32, (STAT, BLOCK), 0)
    stat = jnp.zeros((STAT, BLOCK), F32)
    for i, row in enumerate(rows):
        stat = jnp.where(line == i, jnp.broadcast_to(row, (STAT, BLOCK)), stat)
    for i in range(2 * WINDOW):
        flag = (adj_ref[0, i // WINDOW, i % WINDOW, 0] == 1).astype(jnp.int32).astype(F32)
        stat = jnp.where(line == 8 + i, flag, stat)
    return stat.astype(BF16)


def contract(a, b, da, db):
    return lax.dot_general(a, b, (((da,), (db,)), ((), ())), preferred_element_type=F32)


def unpack_stat(stat, row, slot_flag):
    stat = stat.astype(F32)
    lse = stat[0:1] + stat[1:2] + stat[2:3]
    delta = stat[3:4] + stat[4:5] + stat[5:6]
    keep = slot_flag(stat, 8 + WINDOW * row) > 0.5
    return jnp.where(keep, lse * LOG2E, FAR_AWAY), delta


def flag_of(w):
    return lambda stat, base: stat[base + w:base + w + 1]


def flag_by_parity(odd, w_even, w_odd):
    return lambda stat, base: jnp.where(
        odd == 1, stat[base + w_odd:base + w_odd + 1], stat[base + w_even:base + w_even + 1])


def terms(q, g, k, v, lse, delta):
    scores = contract(k, q, 1, 1) * (SCALE * LOG2E)
    prob = jnp.exp2(scores - lse)
    grad = prob * (contract(v, g, 1, 1) - delta)
    low = prob.astype(BF16)
    grad = grad.astype(BF16)
    dv = contract(low, g, 1, 0)
    dk = contract(grad, q, 1, 0) * SCALE
    dq = contract(grad, k, 0, 0) * SCALE
    return dq, dk, dv

def vmem(shape, dtype):
    return pltpu.VMEM(shape, dtype)


def on_chip(value):
    return pltpu.with_memory_space_constraint(value, pltpu.VMEM)


def call_on_chip(kernel, name, odd, inputs, outs, flops, exps=0, after=None):
    spec = pl.BlockSpec(memory_space=pltpu.VMEM)
    moved_bytes = sum(x.size * x.dtype.itemsize for x in inputs)
    return pl.pallas_call(
        kernel,
        in_specs=[pl.BlockSpec(memory_space=pltpu.SMEM)] + [spec] * len(inputs),
        out_specs=[spec] * len(outs),
        out_shape=[vmem(s, t) for s, t in outs],
        compiler_params=pltpu.CompilerParams(vmem_limit_bytes=16 * 2**20),
        cost_estimate=pl.CostEstimate(flops=flops, bytes_accessed=moved_bytes, transcendentals=exps),
        name=name,
    )(odd, *[on_chip(x) for x in inputs])


def arrived_kernel(odd_ref, *refs):
    refs[-1][0] = odd_ref[0]


def arrived(odd, *inputs):
    spec = pl.BlockSpec(memory_space=pltpu.VMEM)
    smem = pl.BlockSpec(memory_space=pltpu.SMEM)
    return pl.pallas_call(
        arrived_kernel,
        in_specs=[smem] + [spec] * len(inputs),
        out_specs=smem,
        out_shape=jax.ShapeDtypeStruct((1,), jnp.int32),
        compiler_params=pltpu.CompilerParams(vmem_limit_bytes=2**20),
        cost_estimate=pl.CostEstimate(flops=WAIT_FLOPS, bytes_accessed=2**20, transcendentals=0),
        name="arrived",
    )(odd, *[on_chip(x) for x in inputs])


WAIT_FLOPS = 10**11
PACK_STEP = 4


def pack_kernel(odd_ref, adj_ref, lse_ref, q_hbm, k_hbm, v_hbm, o_hbm, g_hbm,
                xqa, xka, xqb, xkb, cross, q_in, k_in, v_in, o_in, g_in, sems):
    width = PACK_STEP * HEAD_DIM
    chunks = 2 * HALF // PACK_STEP
    copies = []
    for c in range(chunks):
        cols = pl.ds(c * width, width)
        copies.append([
            pltpu.make_async_copy(a.at[:, cols], b.at[:, cols], sems.at[c, i])
            for i, (a, b) in enumerate(
                [(q_hbm, q_in), (g_hbm, g_in), (o_hbm, o_in), (k_hbm, k_in), (v_hbm, v_in)])])
        for copy in copies[c]:
            copy.start()
    for c in range(chunks):
        for copy in copies[c]:
            copy.wait()
        for head in range(c * PACK_STEP, (c + 1) * PACK_STEP):
            cols = slice(head * HEAD_DIM, (head + 1) * HEAD_DIM)
            h = head % HALF
            xq, xk = (xqa, xka) if head < HALF else (xqb, xkb)
            xq[h, 0:128, :] = q_in[:, cols]
            xq[h, 128:256, :] = g_in[:, cols]
            xq[h, 256:272, :] = pack_head(adj_ref, g_in[:, cols], o_in[:, cols], lse_ref[head:head + 1])
            xk[h, 0:128, :] = k_in[:, cols]
            xk[h, 128:256, :] = v_in[:, cols]

    is_odd = odd_ref[0] == 1

    @pl.when(is_odd)
    def _():
        cross[...] = xqa[...]

    @pl.when(jnp.logical_not(is_odd))
    def _():
        cross[:, 0:KROWS, :] = xkb[...]
        cross[:, KROWS:QROWS, :] = jnp.zeros((HALF, STAT, HEAD_DIM), BF16)


def pack(odd, adjacency, queries, keys, values, outputs, d_out, row_lse):
    smem = pl.BlockSpec(memory_space=pltpu.SMEM)
    spec = pl.BlockSpec(memory_space=pltpu.VMEM)
    anywhere = pl.BlockSpec(memory_space=pltpu.HBM)
    shapes = [QROWS, KROWS, QROWS, KROWS, QROWS]
    return pl.pallas_call(
        pack_kernel,
        in_specs=[smem, smem, spec] + [anywhere] * 5,
        out_specs=[spec] * len(shapes),
        out_shape=[vmem((HALF, s, HEAD_DIM), BF16) for s in shapes],
        scratch_shapes=[pltpu.VMEM((BLOCK, 2 * HALF * HEAD_DIM), BF16)] * 5
        + [pltpu.SemaphoreType.DMA((2 * HALF // PACK_STEP, 5))],
        compiler_params=pltpu.CompilerParams(vmem_limit_bytes=16 * 2**20),
        cost_estimate=pl.CostEstimate(flops=10**8, bytes_accessed=5 * 2**20, transcendentals=0),
        name="pack",
    )(odd, adjacency, row_lse, *[pltpu.with_memory_space_constraint(x, pltpu.HBM)
                                 for x in (queries, keys, values, outputs, d_out)])


Q3 = slice(0, QROWS)
K3 = slice(QROWS, QROWS + KROWS)
NEAR_Q = slice(QROWS + KROWS, 2 * QROWS + KROWS)
NEAR_K = slice(QROWS + KROWS, QROWS + 2 * KROWS)
MATE_ROWS = 2 * QROWS + KROWS


def mates_kernel(odd_ref, xqa, xkb, q2, k2, out):
    def one_head(h, carry):
        out[h, Q3] = q2[h]
        out[h, K3] = k2[h]
        return carry

    lax.fori_loop(0, HALF, one_head, 0)
    is_odd = odd_ref[0] == 1

    @pl.when(is_odd)
    def _():
        out[:, NEAR_K, :] = xkb[...]
        out[:, NEAR_K.stop:, :] = jnp.zeros((HALF, STAT, HEAD_DIM), BF16)

    @pl.when(jnp.logical_not(is_odd))
    def _():
        out[:, NEAR_Q, :] = xqa[...]


def attend_a_kernel(odd_ref, xqa, cross, q2, mates, xka, fk, swap_b,
                    q_own, q_two, kv_own, swap_out, down_out, far_out):
    odd = odd_ref[0]
    is_odd = odd == 1
    flags = [flag_of(0), flag_by_parity(odd, 3, 1), flag_of(2), flag_by_parity(odd, 1, 3)]

    def one_head(h, carry):
        slots = [xqa[h], jnp.where(is_odd, mates[h, NEAR_Q], cross[h]), q2[h], mates[h, Q3]]
        q = jnp.concatenate([s[0:128] for s in slots], axis=0)
        g = jnp.concatenate([s[128:256] for s in slots], axis=0)
        lse = []
        for row in range(2):
            both = [unpack_stat(s[256:272], row, f) for s, f in zip(slots, flags)]
            lse.append(jnp.broadcast_to(jnp.concatenate([b[0] for b in both], axis=1), (128, 512)))
            delta = jnp.concatenate([b[1] for b in both], axis=1)
        k = jnp.concatenate([xka[h, 0:128], fk[h, 0:128]], axis=0)
        v = jnp.concatenate([xka[h, 128:256], fk[h, 128:256]], axis=0)
        dq, dk, dv = terms(q, g, k, v, jnp.concatenate(lse, axis=0), delta)
        q_own[h] = dq[0:128]
        down_out[h] = dq[128:256].astype(BF16)
        q_two[h] = dq[256:384]
        swap_out[h, 0:128] = dq[384:512].astype(BF16)
        swap_out[h, 128:384] = swap_b[h]
        kv_own[h, 0:128] = dk[0:128]
        kv_own[h, 128:256] = dv[0:128]
        far_out[h, 0:128] = dk[128:256].astype(BF16)
        far_out[h, 128:256] = dv[128:256].astype(BF16)
        return carry

    lax.fori_loop(0, HALF, one_head, 0)


def attend_b_kernel(odd_ref, xkb, cross, k2, mates, xqb, fq,
                    kv_own, kv_two, q_own, swap_out, up_out, far_out):
    odd = odd_ref[0]
    is_odd = odd == 1
    flags = [flag_of(0), flag_by_parity(odd, 1, 3), flag_of(2), flag_by_parity(odd, 3, 1)]

    def one_head(h, carry):
        slots = [xkb[h], jnp.where(is_odd, cross[h, 0:KROWS], mates[h, NEAR_K]), k2[h], mates[h, K3]]
        k = jnp.concatenate([s[0:128] for s in slots], axis=0)
        v = jnp.concatenate([s[128:256] for s in slots], axis=0)
        q = jnp.concatenate([xqb[h, 0:128], fq[h, 0:128]], axis=0)
        g = jnp.concatenate([xqb[h, 128:256], fq[h, 128:256]], axis=0)
        stat_own, stat_far = xqb[h, 256:272], fq[h, 256:272]
        lse = []
        for f in flags:
            own, own_delta = unpack_stat(stat_own, 0, f)
            far, far_delta = unpack_stat(stat_far, 1, f)
            lse.append(jnp.broadcast_to(jnp.concatenate([own, far], axis=1), (128, 256)))
            delta = jnp.concatenate([own_delta, far_delta], axis=1)
        dq, dk, dv = terms(q, g, k, v, jnp.concatenate(lse, axis=0), delta)
        q_own[h] = dq[0:128]
        far_out[h] = dq[128:256].astype(BF16)
        kv_own[h, 0:128] = dk[0:128]
        kv_own[h, 128:256] = dv[0:128]
        up_out[h, 0:128] = dk[128:256].astype(BF16)
        up_out[h, 128:256] = dv[128:256].astype(BF16)
        kv_two[h, 0:128] = dk[256:384]
        kv_two[h, 128:256] = dv[256:384]
        swap_out[h, 0:128] = dk[384:512].astype(BF16)
        swap_out[h, 128:256] = dv[384:512].astype(BF16)
        return carry

    lax.fori_loop(0, HALF, one_head, 0)


def block(rows, dtype):
    return ((HALF, rows, HEAD_DIM), dtype)


def attend_a(odd, *inputs):
    outs = [block(128, F32), block(128, F32), block(256, F32), block(384, BF16), block(128, BF16), block(256, BF16)]
    return call_on_chip(attend_a_kernel, "attend_a", odd, inputs, outs, 13 * 10**8, 2**20)


def attend_b(odd, *inputs):
    outs = [block(256, F32), block(256, F32), block(128, F32), block(256, BF16), block(256, BF16), block(128, BF16)]
    return call_on_chip(attend_b_kernel, "attend_b", odd, inputs, outs, 13 * 10**8, 2**20)


def combine_kernel(parity, rows, odd_ref, mine, swapped, relayed_in, total):
    taken = odd_ref[0] == parity

    def one_head(h, carry):
        relay = jnp.where(taken, relayed_in[h].astype(F32), 0.0)
        total[h] = (mine[h] + swapped[h, rows].astype(F32) + relay).astype(BF16)
        return carry

    lax.fori_loop(0, HALF, one_head, 0)


def combine(parity, rows, name, odd, *inputs):
    return call_on_chip(functools.partial(combine_kernel, parity, rows), name, odd, inputs,
                        [(inputs[0].shape, BF16)], 10**6)[0]


def finish_kernel(odd_ref, q_own, kv_a, down, down_sum, far_k, k_own, q_b, up, up_sum, far_q,
                  dq_hbm, dk_hbm, dv_hbm, dq, dk, dv, sems):
    odd = odd_ref[0]
    copies = []
    for head in range(2 * HALF):
        h = head % HALF
        cols = slice(head * HEAD_DIM, (head + 1) * HEAD_DIM)
        if head < HALF:
            from_down = jnp.where(odd == 1, 0.0, down[h].astype(F32))
            grad_q = q_own[h] + down_sum[h].astype(F32) + from_down
            grad_kv = kv_a[h] + far_k[h].astype(F32)
        else:
            from_up = jnp.where(odd == 1, up[h].astype(F32), 0.0)
            grad_q = q_b[h] + far_q[h].astype(F32)
            grad_kv = k_own[h] + up_sum[h].astype(F32) + from_up
        dq[:, cols] = grad_q.astype(BF16)
        dk[:, cols] = grad_kv[0:128].astype(BF16)
        dv[:, cols] = grad_kv[128:256].astype(BF16)
        if head % PACK_STEP == PACK_STEP - 1:
            c = head // PACK_STEP
            span = pl.ds(c * PACK_STEP * HEAD_DIM, PACK_STEP * HEAD_DIM)
            for i, (a, b) in enumerate([(dq, dq_hbm), (dk, dk_hbm), (dv, dv_hbm)]):
                copies.append(pltpu.make_async_copy(a.at[:, span], b.at[:, span], sems.at[c, i]))
                copies[-1].start()
    for copy in copies:
        copy.wait()


def finish(odd, *inputs):
    spec = pl.BlockSpec(memory_space=pltpu.VMEM)
    whole = (BLOCK, 2 * HALF * HEAD_DIM)
    return pl.pallas_call(
        finish_kernel,
        in_specs=[pl.BlockSpec(memory_space=pltpu.SMEM)] + [spec] * len(inputs),
        out_specs=[pl.BlockSpec(memory_space=pl.ANY)] * 3,
        out_shape=[jax.ShapeDtypeStruct(whole, BF16)] * 3,
        scratch_shapes=[pltpu.VMEM(whole, BF16)] * 3 + [pltpu.SemaphoreType.DMA((2 * HALF // PACK_STEP, 3))],
        compiler_params=pltpu.CompilerParams(vmem_limit_bytes=16 * 2**20),
        cost_estimate=pl.CostEstimate(flops=10**6, bytes_accessed=6 * 2**20, transcendentals=0),
        name="finish",
    )(odd, *[on_chip(x) for x in inputs])


def moved(value, axis, steps):
    count = lax.axis_size(axis)
    return lax.ppermute(value, axis, [(i, (i + steps) % count) for i in range(count)])


def exchanged(value):
    count = lax.axis_size("ka")
    return lax.ppermute(value, "ka", [(i, i ^ 1) for i in range(count)])


def crossed(value):
    count = lax.axis_size("ka")
    return lax.ppermute(value, "ka", [(i, (i + (3 if i % 2 == 1 else -3)) % count) for i in range(count)])


def local(queries, keys, values, outputs, d_out, row_lse, adjacency):
    odd = (lax.axis_index("ka") % 2).astype(jnp.int32).reshape(1)
    xqa, xka, xqb, xkb, cross = pack(odd, adjacency, queries, keys, values, outputs, d_out, row_lse)
    q2 = moved(xqa, "ka", 2)
    k2 = moved(xkb, "ka", -2)
    fq = moved(xqb, "pb", 1)
    fk = moved(xka, "pb", -1)
    cross = crossed(cross)
    mates = exchanged(call_on_chip(mates_kernel, "mates", odd, (xqa, xkb, q2, k2), [block(MATE_ROWS, BF16)], 10**5)[0])
    here = arrived(odd, fq, fk, cross)
    k_own, k_two, q_b, swap_b, up, far_q = attend_b(here, xkb, cross, k2, mates, xqb, fq)
    up = moved(up, "ka", 1)
    far_q = moved(far_q, "pb", -1)
    q_own, q_two, kv_a, swap, down, far_k = attend_a(here, xqa, cross, q2, mates, xka, fk, swap_b)
    down = moved(down, "ka", -1)
    swap = exchanged(swap)
    far_k = moved(far_k, "pb", 1)
    up_sum = moved(combine(0, slice(128, 384), "combine_b", odd, k_two, swap, up), "ka", 2)
    down_sum = moved(combine(1, slice(0, 128), "combine_a", odd, q_two, swap, down), "ka", -2)
    here = arrived(odd, far_q, far_k)
    return tuple(finish(here, q_own, kv_a, down, down_sum, far_k, k_own, q_b, up, up_sum, far_q))


def solution(mesh):
    rows = P(("pb", "ka"), None)
    placed = (rows, rows, rows, rows, rows, P(None, ("pb", "ka")), P(("pb", "ka"), None, None, None))
    return jax.shard_map(
        local,
        mesh=mesh,
        in_specs=placed,
        out_specs=(rows, rows, rows),
        check_vma=False,
    )
```

```python
import functools
import math

import jax
import jax.numpy as jnp
from jax import lax
from jax.experimental import pallas as pl
from jax.experimental.pallas import tpu as pltpu
from jax.sharding import PartitionSpec as P

HEAD_DIM = 128
BLOCK = 128
WINDOW = 4
STAT = 16
HALF = 8
QROWS = 2 * BLOCK + STAT
KROWS = 2 * BLOCK
LOG2E = math.log2(math.e)
SCALE = 1.0 / math.sqrt(HEAD_DIM)
FAR_AWAY = 1e30
F32 = jnp.float32
BF16 = jnp.bfloat16


def three_pieces(value):
    high = value.astype(BF16).astype(F32)
    rest = value - high
    middle = rest.astype(BF16).astype(F32)
    return high, middle, rest - middle


def pack_head(adj_ref, g, o, lse_row):
    down = lax.broadcasted_iota(jnp.int32, (BLOCK, BLOCK), 0)
    across = lax.broadcasted_iota(jnp.int32, (BLOCK, BLOCK), 1)
    product = contract(o, g, 1, 1)
    delta_row = jnp.sum(jnp.where(down == across, product, 0.0), axis=0, keepdims=True)
    rows = list(three_pieces(lse_row)) + list(three_pieces(delta_row))
    line = lax.broadcasted_iota(jnp.int32, (STAT, BLOCK), 0)
    stat = jnp.zeros((STAT, BLOCK), F32)
    for i, row in enumerate(rows):
        stat = jnp.where(line == i, jnp.broadcast_to(row, (STAT, BLOCK)), stat)
    for i in range(2 * WINDOW):
        flag = (adj_ref[0, i // WINDOW, 0, i % WINDOW] == 1).astype(jnp.int32).astype(F32)
        stat = jnp.where(line == 8 + i, flag, stat)
    return stat.astype(BF16)


def contract(a, b, da, db):
    return lax.dot_general(a, b, (((da,), (db,)), ((), ())), preferred_element_type=F32)


def unpack_stat(stat, row, slot_flag):
    stat = stat.astype(F32)
    lse = stat[0:1] + stat[1:2] + stat[2:3]
    delta = stat[3:4] + stat[4:5] + stat[5:6]
    keep = slot_flag(stat, 8 + WINDOW * row) > 0.5
    return jnp.where(keep, lse * LOG2E, FAR_AWAY), delta


def flag_of(w):
    return lambda stat, base: stat[base + w:base + w + 1]


def flag_by_parity(odd, w_even, w_odd):
    return lambda stat, base: jnp.where(
        odd == 1, stat[base + w_odd:base + w_odd + 1], stat[base + w_even:base + w_even + 1])


def terms(q, g, k, v, lse, delta):
    scores = contract(k, q, 1, 1) * (SCALE * LOG2E)
    prob = jnp.exp2(scores - lse)
    grad = prob * (contract(v, g, 1, 1) - delta)
    low = prob.astype(BF16)
    grad = grad.astype(BF16)
    dv = contract(low, g, 1, 0)
    dk = contract(grad, q, 1, 0) * SCALE
    dq = contract(grad, k, 0, 0) * SCALE
    return dq, dk, dv

def vmem(shape, dtype):
    return pltpu.VMEM(shape, dtype)


def on_chip(value):
    return pltpu.with_memory_space_constraint(value, pltpu.VMEM)


def call_on_chip(kernel, name, odd, inputs, outs, flops, exps=0, after=None):
    spec = pl.BlockSpec(memory_space=pltpu.VMEM)
    moved_bytes = sum(x.size * x.dtype.itemsize for x in inputs)
    return pl.pallas_call(
        kernel,
        in_specs=[pl.BlockSpec(memory_space=pltpu.SMEM)] + [spec] * len(inputs),
        out_specs=[spec] * len(outs),
        out_shape=[vmem(s, t) for s, t in outs],
        compiler_params=pltpu.CompilerParams(vmem_limit_bytes=16 * 2**20),
        cost_estimate=pl.CostEstimate(flops=flops, bytes_accessed=moved_bytes, transcendentals=exps),
        name=name,
    )(odd, *[on_chip(x) for x in inputs])


def arrived_kernel(odd_ref, *refs):
    refs[-1][0] = odd_ref[0]


def arrived(odd, *inputs):
    spec = pl.BlockSpec(memory_space=pltpu.VMEM)
    smem = pl.BlockSpec(memory_space=pltpu.SMEM)
    return pl.pallas_call(
        arrived_kernel,
        in_specs=[smem] + [spec] * len(inputs),
        out_specs=smem,
        out_shape=jax.ShapeDtypeStruct((1,), jnp.int32),
        compiler_params=pltpu.CompilerParams(vmem_limit_bytes=2**20),
        cost_estimate=pl.CostEstimate(flops=WAIT_FLOPS, bytes_accessed=2**20, transcendentals=0),
        name="arrived",
    )(odd, *[on_chip(x) for x in inputs])


WAIT_FLOPS = 10**11
PACK_STEP = 4


def pack_kernel(odd_ref, adj_ref, lse_hbm, q_hbm, k_hbm, v_hbm, o_hbm, g_hbm,
                xqa, xka, xqb, xkb, cross, q_in, k_in, v_in, o_in, g_in, lse_ref, sems, lse_sem):
    lse_copy = pltpu.make_async_copy(lse_hbm, lse_ref, lse_sem)
    lse_copy.start()
    width = PACK_STEP * HEAD_DIM
    chunks = 2 * HALF // PACK_STEP
    copies = []
    for c in range(chunks):
        cols = pl.ds(c * width, width)
        copies.append([
            pltpu.make_async_copy(a.at[:, cols], b.at[:, cols], sems.at[c, i])
            for i, (a, b) in enumerate(
                [(q_hbm, q_in), (g_hbm, g_in), (o_hbm, o_in), (k_hbm, k_in), (v_hbm, v_in)])])
        for copy in copies[c]:
            copy.start()
    lse_copy.wait()
    for c in range(chunks):
        for copy in copies[c]:
            copy.wait()
        for head in range(c * PACK_STEP, (c + 1) * PACK_STEP):
            cols = slice(head * HEAD_DIM, (head + 1) * HEAD_DIM)
            h = head % HALF
            xq, xk = (xqa, xka) if head < HALF else (xqb, xkb)
            xq[h, 0:128, :] = q_in[:, cols]
            xq[h, 128:256, :] = g_in[:, cols]
            xq[h, 256:272, :] = pack_head(adj_ref, g_in[:, cols], o_in[:, cols], lse_ref[head:head + 1])
            xk[h, 0:128, :] = k_in[:, cols]
            xk[h, 128:256, :] = v_in[:, cols]

    is_odd = odd_ref[0] == 1

    @pl.when(is_odd)
    def _():
        cross[...] = xqa[...]

    @pl.when(jnp.logical_not(is_odd))
    def _():
        cross[:, 0:KROWS, :] = xkb[...]
        cross[:, KROWS:QROWS, :] = jnp.zeros((HALF, STAT, HEAD_DIM), BF16)


def pack(odd, adjacency, queries, keys, values, outputs, d_out, row_lse):
    smem = pl.BlockSpec(memory_space=pltpu.SMEM)
    spec = pl.BlockSpec(memory_space=pltpu.VMEM)
    anywhere = pl.BlockSpec(memory_space=pltpu.HBM)
    shapes = [QROWS, KROWS, QROWS, KROWS, QROWS]
    return pl.pallas_call(
        pack_kernel,
        in_specs=[smem, smem] + [anywhere] * 6,
        out_specs=[spec] * len(shapes),
        out_shape=[vmem((HALF, s, HEAD_DIM), BF16) for s in shapes],
        scratch_shapes=[pltpu.VMEM((BLOCK, 2 * HALF * HEAD_DIM), BF16)] * 5
        + [pltpu.VMEM((2 * HALF, BLOCK), F32), pltpu.SemaphoreType.DMA((2 * HALF // PACK_STEP, 5)),
           pltpu.SemaphoreType.DMA],
        compiler_params=pltpu.CompilerParams(vmem_limit_bytes=16 * 2**20),
        cost_estimate=pl.CostEstimate(flops=10**8, bytes_accessed=5 * 2**20, transcendentals=0),
        name="pack",
    )(odd, adjacency, *[pltpu.with_memory_space_constraint(x, pltpu.HBM)
                        for x in (row_lse, queries, keys, values, outputs, d_out)])


Q3 = slice(0, QROWS)
K3 = slice(QROWS, QROWS + KROWS)
NEAR_Q = slice(QROWS + KROWS, 2 * QROWS + KROWS)
NEAR_K = slice(QROWS + KROWS, QROWS + 2 * KROWS)
MATE_ROWS = 2 * QROWS + KROWS


def mates_kernel(odd_ref, xqa, xkb, q2, k2, out):
    def one_head(h, carry):
        out[h, Q3] = q2[h]
        out[h, K3] = k2[h]
        return carry

    lax.fori_loop(0, HALF, one_head, 0)
    is_odd = odd_ref[0] == 1

    @pl.when(is_odd)
    def _():
        out[:, NEAR_K, :] = xkb[...]
        out[:, NEAR_K.stop:, :] = jnp.zeros((HALF, STAT, HEAD_DIM), BF16)

    @pl.when(jnp.logical_not(is_odd))
    def _():
        out[:, NEAR_Q, :] = xqa[...]


def attend_a_kernel(odd_ref, xqa, cross, q2, mates, xka, fk,
                    q_own, q_two, kv_own, swap_out, down_out, far_out):
    odd = odd_ref[0]
    is_odd = odd == 1
    flags = [flag_of(0), flag_by_parity(odd, 3, 1), flag_of(2), flag_by_parity(odd, 1, 3)]

    def one_head(h, carry):
        slots = [xqa[h], jnp.where(is_odd, mates[h, NEAR_Q], cross[h]), q2[h], mates[h, Q3]]
        q = jnp.concatenate([s[0:128] for s in slots], axis=0)
        g = jnp.concatenate([s[128:256] for s in slots], axis=0)
        lse = []
        for row in range(2):
            both = [unpack_stat(s[256:272], row, f) for s, f in zip(slots, flags)]
            lse.append(jnp.broadcast_to(jnp.concatenate([b[0] for b in both], axis=1), (128, 512)))
            delta = jnp.concatenate([b[1] for b in both], axis=1)
        k = jnp.concatenate([xka[h, 0:128], fk[h, 0:128]], axis=0)
        v = jnp.concatenate([xka[h, 128:256], fk[h, 128:256]], axis=0)
        dq, dk, dv = terms(q, g, k, v, jnp.concatenate(lse, axis=0), delta)
        q_own[h] = dq[0:128]
        down_out[h] = dq[128:256].astype(BF16)
        q_two[h] = dq[256:384]
        swap_out[h] = dq[384:512].astype(BF16)
        kv_own[h, 0:128] = dk[0:128]
        kv_own[h, 128:256] = dv[0:128]
        far_out[h, 0:128] = dk[128:256].astype(BF16)
        far_out[h, 128:256] = dv[128:256].astype(BF16)
        return carry

    lax.fori_loop(0, HALF, one_head, 0)


def attend_b_kernel(odd_ref, xkb, cross, k2, mates, xqb, fq,
                    kv_own, kv_two, q_own, swap_out, up_out, far_out):
    odd = odd_ref[0]
    is_odd = odd == 1
    flags = [flag_of(0), flag_by_parity(odd, 1, 3), flag_of(2), flag_by_parity(odd, 3, 1)]

    def one_head(h, carry):
        slots = [xkb[h], jnp.where(is_odd, cross[h, 0:KROWS], mates[h, NEAR_K]), k2[h], mates[h, K3]]
        k = jnp.concatenate([s[0:128] for s in slots], axis=0)
        v = jnp.concatenate([s[128:256] for s in slots], axis=0)
        q = jnp.concatenate([xqb[h, 0:128], fq[h, 0:128]], axis=0)
        g = jnp.concatenate([xqb[h, 128:256], fq[h, 128:256]], axis=0)
        stat_own, stat_far = xqb[h, 256:272], fq[h, 256:272]
        lse = []
        for f in flags:
            own, own_delta = unpack_stat(stat_own, 0, f)
            far, far_delta = unpack_stat(stat_far, 1, f)
            lse.append(jnp.broadcast_to(jnp.concatenate([own, far], axis=1), (128, 256)))
            delta = jnp.concatenate([own_delta, far_delta], axis=1)
        dq, dk, dv = terms(q, g, k, v, jnp.concatenate(lse, axis=0), delta)
        q_own[h] = dq[0:128]
        far_out[h] = dq[128:256].astype(BF16)
        kv_own[h, 0:128] = dk[0:128]
        kv_own[h, 128:256] = dv[0:128]
        up_out[h, 0:128] = dk[128:256].astype(BF16)
        up_out[h, 128:256] = dv[128:256].astype(BF16)
        kv_two[h, 0:128] = dk[256:384]
        kv_two[h, 128:256] = dv[256:384]
        swap_out[h, 0:128] = dk[384:512].astype(BF16)
        swap_out[h, 128:256] = dv[384:512].astype(BF16)
        return carry

    lax.fori_loop(0, HALF, one_head, 0)


def block(rows, dtype):
    return ((HALF, rows, HEAD_DIM), dtype)


def attend_a(odd, *inputs):
    outs = [block(128, F32), block(128, F32), block(256, F32), block(128, BF16), block(128, BF16), block(256, BF16)]
    return call_on_chip(attend_a_kernel, "attend_a", odd, inputs, outs, 13 * 10**8, 2**20)


def attend_b(odd, *inputs):
    outs = [block(256, F32), block(256, F32), block(128, F32), block(256, BF16), block(256, BF16), block(128, BF16)]
    return call_on_chip(attend_b_kernel, "attend_b", odd, inputs, outs, 13 * 10**8, 2**20)


def combine_kernel(odd_ref, mine, swapped, total):
    def one_head(h, carry):
        total[h] = (mine[h] + swapped[h].astype(F32)).astype(BF16)
        return carry

    lax.fori_loop(0, HALF, one_head, 0)


def combine(name, odd, *inputs):
    return call_on_chip(combine_kernel, name, odd, inputs, [(inputs[0].shape, BF16)], 10**6)[0]


def finish_kernel(odd_ref, q_own, kv_a, down, down_sum, far_k, k_own, q_b, up, up_sum, far_q,
                  dq_hbm, dk_hbm, dv_hbm, dq, dk, dv, sems):
    copies = []
    for head in range(2 * HALF):
        h = head % HALF
        cols = slice(head * HEAD_DIM, (head + 1) * HEAD_DIM)
        if head < HALF:
            grad_q = q_own[h] + down_sum[h].astype(F32) + down[h].astype(F32)
            grad_kv = kv_a[h] + far_k[h].astype(F32)
        else:
            grad_q = q_b[h] + far_q[h].astype(F32)
            grad_kv = k_own[h] + up_sum[h].astype(F32) + up[h].astype(F32)
        dq[:, cols] = grad_q.astype(BF16)
        dk[:, cols] = grad_kv[0:128].astype(BF16)
        dv[:, cols] = grad_kv[128:256].astype(BF16)
        if head % PACK_STEP == PACK_STEP - 1:
            c = head // PACK_STEP
            span = pl.ds(c * PACK_STEP * HEAD_DIM, PACK_STEP * HEAD_DIM)
            for i, (a, b) in enumerate([(dq, dq_hbm), (dk, dk_hbm), (dv, dv_hbm)]):
                copies.append(pltpu.make_async_copy(a.at[:, span], b.at[:, span], sems.at[c, i]))
                copies[-1].start()
    for copy in copies:
        copy.wait()


def finish(odd, *inputs):
    spec = pl.BlockSpec(memory_space=pltpu.VMEM)
    whole = (BLOCK, 2 * HALF * HEAD_DIM)
    return pl.pallas_call(
        finish_kernel,
        in_specs=[pl.BlockSpec(memory_space=pltpu.SMEM)] + [spec] * len(inputs),
        out_specs=[pl.BlockSpec(memory_space=pl.ANY)] * 3,
        out_shape=[jax.ShapeDtypeStruct(whole, BF16)] * 3,
        scratch_shapes=[pltpu.VMEM(whole, BF16)] * 3 + [pltpu.SemaphoreType.DMA((2 * HALF // PACK_STEP, 3))],
        compiler_params=pltpu.CompilerParams(vmem_limit_bytes=16 * 2**20),
        cost_estimate=pl.CostEstimate(flops=10**6, bytes_accessed=6 * 2**20, transcendentals=0),
        name="finish",
    )(odd, *[on_chip(x) for x in inputs])


def moved(value, axis, steps):
    count = lax.axis_size(axis)
    return lax.ppermute(value, axis, [(i, (i + steps) % count) for i in range(count)])


def exchanged(value):
    count = lax.axis_size("ka")
    return lax.ppermute(value, "ka", [(i, i ^ 1) for i in range(count)])


def crossed(value, odd_steps, even_steps):
    count = lax.axis_size("ka")
    return lax.ppermute(
        value, "ka", [(i, (i + (odd_steps if i % 2 == 1 else even_steps)) % count) for i in range(count)])


def local(queries, keys, values, outputs, d_out, row_lse, adjacency):
    odd = (lax.axis_index("ka") % 2).astype(jnp.int32).reshape(1)
    xqa, xka, xqb, xkb, cross = pack(
        odd, adjacency.transpose(0, 1, 3, 2), queries, keys, values, outputs, d_out, row_lse)
    fq = moved(xqb, "pb", 1)
    q2 = moved(xqa, "ka", 2)
    k2 = moved(xkb, "ka", -2)
    cross = crossed(cross, 3, -3)
    mates = call_on_chip(mates_kernel, "mates", odd, (xqa, xkb, q2, k2), [block(MATE_ROWS, BF16)], 10**5)[0]
    mates, xka = lax.optimization_barrier((mates, xka))
    mates = exchanged(mates)
    fk = moved(xka, "pb", -1)
    here = arrived(odd, fq, cross)
    k_own, k_two, q_b, swap_b, up, far_q = attend_b(here, xkb, cross, k2, mates, xqb, fq)
    up = crossed(up, 3, 1)
    far_q = moved(far_q, "pb", -1)
    swap_b, fk = lax.optimization_barrier((exchanged(swap_b), fk))
    b_sum = combine("combine_b", odd, k_two, swap_b)
    xka, b_sum = lax.optimization_barrier((xka, b_sum))
    up_sum = moved(b_sum, "ka", 2)
    q_own, q_two, kv_a, swap_a, down, far_k = attend_a(here, xqa, cross, q2, mates, xka, fk)
    down, swap_a, far_k, far_q = lax.optimization_barrier((down, swap_a, far_k, far_q))
    down = crossed(down, -1, -3)
    far_k = moved(far_k, "pb", 1)
    down_sum = moved(combine("combine_a", odd, q_two, exchanged(swap_a)), "ka", -2)
    here = arrived(odd, far_q, up, up_sum)
    return tuple(finish(here, q_own, kv_a, down, down_sum, far_k, k_own, q_b, up, up_sum, far_q))


def solution(mesh):
    rows = P(("pb", "ka"), None)
    placed = (rows, rows, rows, rows, rows, P(None, ("pb", "ka")), P(("pb", "ka"), None, None, None))
    return jax.shard_map(
        local,
        mesh=mesh,
        in_specs=placed,
        out_specs=(rows, rows, rows),
        check_vma=False,
    )
```

```python
import functools
import math

import jax
import jax.numpy as jnp
from jax import lax
from jax.experimental import pallas as pl
from jax.experimental.pallas import tpu as pltpu
from jax.sharding import PartitionSpec as P

HEAD_DIM = 128
BLOCK = 128
WINDOW = 4
STAT = 16
HALF = 8
QROWS = 2 * BLOCK + STAT
KROWS = 2 * BLOCK
LOG2E = math.log2(math.e)
SCALE = 1.0 / math.sqrt(HEAD_DIM)
FAR_AWAY = 1e30
F32 = jnp.float32
BF16 = jnp.bfloat16


def three_pieces(value):
    high = value.astype(BF16).astype(F32)
    rest = value - high
    middle = rest.astype(BF16).astype(F32)
    return high, middle, rest - middle


def pack_head(adj_ref, g, o, lse_row):
    down = lax.broadcasted_iota(jnp.int32, (BLOCK, BLOCK), 0)
    across = lax.broadcasted_iota(jnp.int32, (BLOCK, BLOCK), 1)
    product = contract(o, g, 1, 1)
    delta_row = jnp.sum(jnp.where(down == across, product, 0.0), axis=0, keepdims=True)
    rows = list(three_pieces(lse_row)) + list(three_pieces(delta_row))
    line = lax.broadcasted_iota(jnp.int32, (STAT, BLOCK), 0)
    stat = jnp.zeros((STAT, BLOCK), F32)
    for i, row in enumerate(rows):
        stat = jnp.where(line == i, jnp.broadcast_to(row, (STAT, BLOCK)), stat)
    for i in range(2 * WINDOW):
        flag = (adj_ref[0, i // WINDOW, 0, i % WINDOW] == 1).astype(jnp.int32).astype(F32)
        stat = jnp.where(line == 8 + i, flag, stat)
    return stat.astype(BF16)


def contract(a, b, da, db):
    return lax.dot_general(a, b, (((da,), (db,)), ((), ())), preferred_element_type=F32)


def unpack_stat(stat, row, slot_flag):
    stat = stat.astype(F32)
    lse = stat[0:1] + stat[1:2] + stat[2:3]
    delta = stat[3:4] + stat[4:5] + stat[5:6]
    keep = slot_flag(stat, 8 + WINDOW * row) > 0.5
    return jnp.where(keep, lse * LOG2E, FAR_AWAY), delta


def flag_of(w):
    return lambda stat, base: stat[base + w:base + w + 1]


def flag_by_parity(odd, w_even, w_odd):
    return lambda stat, base: jnp.where(
        odd == 1, stat[base + w_odd:base + w_odd + 1], stat[base + w_even:base + w_even + 1])


def terms(q, g, k, v, lse, delta):
    scores = contract(k, q, 1, 1) * (SCALE * LOG2E)
    prob = jnp.exp2(scores - lse)
    grad = prob * (contract(v, g, 1, 1) - delta)
    low = prob.astype(BF16)
    grad = grad.astype(BF16)
    dv = contract(low, g, 1, 0)
    dk = contract(grad, q, 1, 0) * SCALE
    dq = contract(grad, k, 0, 0) * SCALE
    return dq, dk, dv

def vmem(shape, dtype):
    return pltpu.VMEM(shape, dtype)


def on_chip(value):
    return pltpu.with_memory_space_constraint(value, pltpu.VMEM)


def call_on_chip(kernel, name, odd, inputs, outs, flops, exps=0, after=None):
    spec = pl.BlockSpec(memory_space=pltpu.VMEM)
    moved_bytes = sum(x.size * x.dtype.itemsize for x in inputs)
    return pl.pallas_call(
        kernel,
        in_specs=[pl.BlockSpec(memory_space=pltpu.SMEM)] + [spec] * len(inputs),
        out_specs=[spec] * len(outs),
        out_shape=[vmem(s, t) for s, t in outs],
        compiler_params=pltpu.CompilerParams(vmem_limit_bytes=16 * 2**20),
        cost_estimate=pl.CostEstimate(flops=flops, bytes_accessed=moved_bytes, transcendentals=exps),
        name=name,
    )(odd, *[on_chip(x) for x in inputs])


def arrived_kernel(odd_ref, *refs):
    refs[-1][0] = odd_ref[0]


def arrived(odd, *inputs):
    spec = pl.BlockSpec(memory_space=pltpu.VMEM)
    smem = pl.BlockSpec(memory_space=pltpu.SMEM)
    return pl.pallas_call(
        arrived_kernel,
        in_specs=[smem] + [spec] * len(inputs),
        out_specs=smem,
        out_shape=jax.ShapeDtypeStruct((1,), jnp.int32),
        compiler_params=pltpu.CompilerParams(vmem_limit_bytes=2**20),
        cost_estimate=pl.CostEstimate(flops=WAIT_FLOPS, bytes_accessed=2**20, transcendentals=0),
        name="arrived",
    )(odd, *[on_chip(x) for x in inputs])


WAIT_FLOPS = 10**11
PACK_STEP = 4


def pack_kernel(odd_ref, adj_hbm, lse_hbm, q_hbm, k_hbm, v_hbm, o_hbm, g_hbm,
                xqa, xka, xqb, xkb, cross, q_in, k_in, v_in, o_in, g_in, lse_ref, adj_ref, sems, lse_sem, adj_sem):
    adj_copy = pltpu.make_async_copy(adj_hbm, adj_ref, adj_sem)
    adj_copy.start()
    lse_copy = pltpu.make_async_copy(lse_hbm, lse_ref, lse_sem)
    lse_copy.start()
    width = PACK_STEP * HEAD_DIM
    chunks = 2 * HALF // PACK_STEP
    copies = []
    for c in range(chunks):
        cols = pl.ds(c * width, width)
        copies.append([
            pltpu.make_async_copy(a.at[:, cols], b.at[:, cols], sems.at[c, i])
            for i, (a, b) in enumerate(
                [(q_hbm, q_in), (g_hbm, g_in), (o_hbm, o_in), (k_hbm, k_in), (v_hbm, v_in)])])
        for copy in copies[c]:
            copy.start()
    adj_copy.wait()
    lse_copy.wait()
    for c in range(chunks):
        for copy in copies[c]:
            copy.wait()
        for head in range(c * PACK_STEP, (c + 1) * PACK_STEP):
            cols = slice(head * HEAD_DIM, (head + 1) * HEAD_DIM)
            h = head % HALF
            xq, xk = (xqa, xka) if head < HALF else (xqb, xkb)
            xq[h, 0:128, :] = q_in[:, cols]
            xq[h, 128:256, :] = g_in[:, cols]
            xq[h, 256:272, :] = pack_head(adj_ref, g_in[:, cols], o_in[:, cols], lse_ref[head:head + 1])
            xk[h, 0:128, :] = k_in[:, cols]
            xk[h, 128:256, :] = v_in[:, cols]

    is_odd = odd_ref[0] == 1

    @pl.when(is_odd)
    def _():
        cross[...] = xqa[...]

    @pl.when(jnp.logical_not(is_odd))
    def _():
        cross[:, 0:KROWS, :] = xkb[...]
        cross[:, KROWS:QROWS, :] = jnp.zeros((HALF, STAT, HEAD_DIM), BF16)


def pack(odd, adjacency, queries, keys, values, outputs, d_out, row_lse):
    smem = pl.BlockSpec(memory_space=pltpu.SMEM)
    spec = pl.BlockSpec(memory_space=pltpu.VMEM)
    anywhere = pl.BlockSpec(memory_space=pltpu.HBM)
    shapes = [QROWS, KROWS, QROWS, KROWS, QROWS]
    return pl.pallas_call(
        pack_kernel,
        in_specs=[smem] + [anywhere] * 7,
        out_specs=[spec] * len(shapes),
        out_shape=[vmem((HALF, s, HEAD_DIM), BF16) for s in shapes],
        scratch_shapes=[pltpu.VMEM((BLOCK, 2 * HALF * HEAD_DIM), BF16)] * 5
        + [pltpu.VMEM((2 * HALF, BLOCK), F32), pltpu.SMEM((1, 2, 1, WINDOW), jnp.int32),
           pltpu.SemaphoreType.DMA((2 * HALF // PACK_STEP, 5)), pltpu.SemaphoreType.DMA, pltpu.SemaphoreType.DMA],
        compiler_params=pltpu.CompilerParams(vmem_limit_bytes=16 * 2**20),
        cost_estimate=pl.CostEstimate(flops=10**8, bytes_accessed=5 * 2**20, transcendentals=0),
        name="pack",
    )(odd, *[pltpu.with_memory_space_constraint(x, pltpu.HBM)
             for x in (adjacency, row_lse, queries, keys, values, outputs, d_out)])


Q3 = slice(0, QROWS)
K3 = slice(QROWS, QROWS + KROWS)
NEAR_Q = slice(QROWS + KROWS, 2 * QROWS + KROWS)
NEAR_K = slice(QROWS + KROWS, QROWS + 2 * KROWS)
MATE_ROWS = 2 * QROWS + KROWS


def mates_kernel(odd_ref, xqa, xkb, q2, k2, out):
    def one_head(h, carry):
        out[h, Q3] = q2[h]
        out[h, K3] = k2[h]
        return carry

    lax.fori_loop(0, HALF, one_head, 0)
    is_odd = odd_ref[0] == 1

    @pl.when(is_odd)
    def _():
        out[:, NEAR_K, :] = xkb[...]
        out[:, NEAR_K.stop:, :] = jnp.zeros((HALF, STAT, HEAD_DIM), BF16)

    @pl.when(jnp.logical_not(is_odd))
    def _():
        out[:, NEAR_Q, :] = xqa[...]


def attend_a_kernel(odd_ref, xqa, cross, q2, mates, xka, fk,
                    q_own, q_two, kv_own, swap_out, down_out, far_out):
    odd = odd_ref[0]
    is_odd = odd == 1
    flags = [flag_of(0), flag_by_parity(odd, 3, 1), flag_of(2), flag_by_parity(odd, 1, 3)]

    def one_head(h, carry):
        slots = [xqa[h], jnp.where(is_odd, mates[h, NEAR_Q], cross[h]), q2[h], mates[h, Q3]]
        q = jnp.concatenate([s[0:128] for s in slots], axis=0)
        g = jnp.concatenate([s[128:256] for s in slots], axis=0)
        lse = []
        for row in range(2):
            both = [unpack_stat(s[256:272], row, f) for s, f in zip(slots, flags)]
            lse.append(jnp.broadcast_to(jnp.concatenate([b[0] for b in both], axis=1), (128, 512)))
            delta = jnp.concatenate([b[1] for b in both], axis=1)
        k = jnp.concatenate([xka[h, 0:128], fk[h, 0:128]], axis=0)
        v = jnp.concatenate([xka[h, 128:256], fk[h, 128:256]], axis=0)
        dq, dk, dv = terms(q, g, k, v, jnp.concatenate(lse, axis=0), delta)
        q_own[h] = dq[0:128]
        down_out[h] = dq[128:256].astype(BF16)
        q_two[h] = dq[256:384]
        swap_out[h] = dq[384:512].astype(BF16)
        kv_own[h, 0:128] = dk[0:128]
        kv_own[h, 128:256] = dv[0:128]
        far_out[h, 0:128] = dk[128:256].astype(BF16)
        far_out[h, 128:256] = dv[128:256].astype(BF16)
        return carry

    lax.fori_loop(0, HALF, one_head, 0, unroll=4)


def attend_b_kernel(odd_ref, xkb, cross, k2, mates, xqb, fq,
                    kv_own, kv_two, q_own, swap_out, up_out, far_out):
    odd = odd_ref[0]
    is_odd = odd == 1
    flags = [flag_of(0), flag_by_parity(odd, 1, 3), flag_of(2), flag_by_parity(odd, 3, 1)]

    def one_head(h, carry):
        slots = [xkb[h], jnp.where(is_odd, cross[h, 0:KROWS], mates[h, NEAR_K]), k2[h], mates[h, K3]]
        k = jnp.concatenate([s[0:128] for s in slots], axis=0)
        v = jnp.concatenate([s[128:256] for s in slots], axis=0)
        q = jnp.concatenate([xqb[h, 0:128], fq[h, 0:128]], axis=0)
        g = jnp.concatenate([xqb[h, 128:256], fq[h, 128:256]], axis=0)
        stat_own, stat_far = xqb[h, 256:272], fq[h, 256:272]
        lse = []
        for f in flags:
            own, own_delta = unpack_stat(stat_own, 0, f)
            far, far_delta = unpack_stat(stat_far, 1, f)
            lse.append(jnp.broadcast_to(jnp.concatenate([own, far], axis=1), (128, 256)))
            delta = jnp.concatenate([own_delta, far_delta], axis=1)
        dq, dk, dv = terms(q, g, k, v, jnp.concatenate(lse, axis=0), delta)
        q_own[h] = dq[0:128]
        far_out[h] = dq[128:256].astype(BF16)
        kv_own[h, 0:128] = dk[0:128]
        kv_own[h, 128:256] = dv[0:128]
        up_out[h, 0:128] = dk[128:256].astype(BF16)
        up_out[h, 128:256] = dv[128:256].astype(BF16)
        kv_two[h, 0:128] = dk[256:384]
        kv_two[h, 128:256] = dv[256:384]
        swap_out[h, 0:128] = dk[384:512].astype(BF16)
        swap_out[h, 128:256] = dv[384:512].astype(BF16)
        return carry

    lax.fori_loop(0, HALF, one_head, 0, unroll=4)


def block(rows, dtype):
    return ((HALF, rows, HEAD_DIM), dtype)


def attend_a(odd, *inputs):
    outs = [block(128, F32), block(128, F32), block(256, F32), block(128, BF16), block(128, BF16), block(256, BF16)]
    return call_on_chip(attend_a_kernel, "attend_a", odd, inputs, outs, 13 * 10**8, 2**20)


def attend_b(odd, *inputs):
    outs = [block(256, F32), block(256, F32), block(128, F32), block(256, BF16), block(256, BF16), block(128, BF16)]
    return call_on_chip(attend_b_kernel, "attend_b", odd, inputs, outs, 13 * 10**8, 2**20)


def combine_kernel(odd_ref, mine, swapped, total):
    def one_head(h, carry):
        total[h] = (mine[h] + swapped[h].astype(F32)).astype(BF16)
        return carry

    lax.fori_loop(0, HALF, one_head, 0)


def combine(name, odd, *inputs):
    return call_on_chip(combine_kernel, name, odd, inputs, [(inputs[0].shape, BF16)], 10**6)[0]


def finish_kernel(first, grads, outs, stage, sems):
    copies = []
    step = 2
    for h in range(HALF):
        cols = slice(h * HEAD_DIM, (h + 1) * HEAD_DIM)
        for part, grad in zip(stage, grads(h)):
            part[:, cols] = grad.astype(BF16)
        if h % step == step - 1:
            c = h // step
            width = step * HEAD_DIM
            for i, (part, out) in enumerate(zip(stage, outs)):
                copies.append(pltpu.make_async_copy(
                    part.at[:, pl.ds(c * width, width)],
                    out.at[:, pl.ds(first * HEAD_DIM + c * width, width)], sems.at[c, i]))
                copies[-1].start()
    for copy in copies:
        copy.wait()


def finish_b_kernel(k_own, q_b, up, up_sum, far_q, dq, dk, dv, *scratch):
    def grads(h):
        kv = k_own[h] + up_sum[h].astype(F32) + up[h].astype(F32)
        return q_b[h] + far_q[h].astype(F32), kv[0:128], kv[128:256]

    finish_kernel(HALF, grads, (dq, dk, dv), scratch[0:3], scratch[3])


def finish_a_kernel(q_own, kv_a, down, down_sum, far_k, dq_in, dk_in, dv_in, dq, dk, dv, *scratch):
    def grads(h):
        kv = kv_a[h] + far_k[h].astype(F32)
        return q_own[h] + down_sum[h].astype(F32) + down[h].astype(F32), kv[0:128], kv[128:256]

    finish_kernel(0, grads, (dq, dk, dv), scratch[0:3], scratch[3])


def finish(kernel, name, flops, inputs, partial=()):
    spec = pl.BlockSpec(memory_space=pltpu.VMEM)
    anywhere = pl.BlockSpec(memory_space=pltpu.HBM)
    whole = jax.ShapeDtypeStruct((BLOCK, 2 * HALF * HEAD_DIM), BF16)
    return pl.pallas_call(
        kernel,
        in_specs=[spec] * len(inputs) + [anywhere] * len(partial),
        out_specs=[anywhere] * 3,
        out_shape=[whole] * 3,
        input_output_aliases={len(inputs) + i: i for i in range(len(partial))},
        scratch_shapes=[pltpu.VMEM((BLOCK, HALF * HEAD_DIM), BF16)] * 3 + [pltpu.SemaphoreType.DMA((HALF // 2, 3))],
        compiler_params=pltpu.CompilerParams(vmem_limit_bytes=8 * 2**20),
        cost_estimate=pl.CostEstimate(flops=flops, bytes_accessed=3 * 2**20, transcendentals=0),
        name=name,
    )(*[on_chip(x) for x in inputs], *partial)


def moved(value, axis, steps):
    count = lax.axis_size(axis)
    return lax.ppermute(value, axis, [(i, (i + steps) % count) for i in range(count)])


def exchanged(value):
    count = lax.axis_size("ka")
    return lax.ppermute(value, "ka", [(i, i ^ 1) for i in range(count)])


def crossed(value, odd_steps, even_steps):
    count = lax.axis_size("ka")
    return lax.ppermute(
        value, "ka", [(i, (i + (odd_steps if i % 2 == 1 else even_steps)) % count) for i in range(count)])


def local(queries, keys, values, outputs, d_out, row_lse, adjacency):
    odd = (lax.axis_index("ka") % 2).astype(jnp.int32).reshape(1)
    xqa, xka, xqb, xkb, cross = pack(
        odd, adjacency.transpose(0, 1, 3, 2), queries, keys, values, outputs, d_out, row_lse)
    fq = moved(xqb, "pb", 1)
    q2 = moved(xqa, "ka", 2)
    k2 = moved(xkb, "ka", -2)
    cross = crossed(cross, 3, -3)
    mates = call_on_chip(mates_kernel, "mates", odd, (xqa, xkb, q2, k2), [block(MATE_ROWS, BF16)], 10**5)[0]
    mates, xka = lax.optimization_barrier((mates, xka))
    mates = exchanged(mates)
    fk = moved(xka, "pb", -1)
    here = arrived(odd, fq, cross)
    k_own, k_two, q_b, swap_b, up, far_q = attend_b(here, xkb, cross, k2, mates, xqb, fq)
    up = crossed(up, 3, 1)
    far_q = moved(far_q, "pb", -1)
    swap_b, fk = lax.optimization_barrier((exchanged(swap_b), fk))
    b_sum = combine("combine_b", odd, k_two, swap_b)
    xka, b_sum = lax.optimization_barrier((xka, b_sum))
    up_sum = moved(b_sum, "ka", 2)
    q_own, q_two, kv_a, swap_a, down, far_k = attend_a(here, xqa, cross, q2, mates, xka, fk)
    down, swap_a, far_k, far_q = lax.optimization_barrier((down, swap_a, far_k, far_q))
    down = crossed(down, -1, -3)
    far_k = moved(far_k, "pb", 1)
    down_sum = moved(combine("combine_a", odd, q_two, exchanged(swap_a)), "ka", -2)
    grads = finish(finish_b_kernel, "finish_b", WAIT_FLOPS, (k_own, q_b, up, up_sum, far_q))
    return tuple(finish(finish_a_kernel, "finish_a", 10**6, (q_own, kv_a, down, down_sum, far_k), grads))


def solution(mesh):
    rows = P(("pb", "ka"), None)
    placed = (rows, rows, rows, rows, rows, P(None, ("pb", "ka")), P(("pb", "ka"), None, None, None))
    return jax.shard_map(
        local,
        mesh=mesh,
        in_specs=placed,
        out_specs=(rows, rows, rows),
        check_vma=False,
    )
```

```python
import functools
import math

import jax
import jax.numpy as jnp
from jax import lax
from jax.experimental import pallas as pl
from jax.experimental.pallas import tpu as pltpu
from jax.sharding import PartitionSpec as P

HEAD_DIM = 128
BLOCK = 128
WINDOW = 4
STAT = 16
HALF = 8
QROWS = 2 * BLOCK + STAT
KROWS = 2 * BLOCK
LOG2E = math.log2(math.e)
SCALE = 1.0 / math.sqrt(HEAD_DIM)
FAR_AWAY = 1e30
F32 = jnp.float32
BF16 = jnp.bfloat16


def three_pieces(value):
    high = value.astype(BF16).astype(F32)
    rest = value - high
    middle = rest.astype(BF16).astype(F32)
    return high, middle, rest - middle


def flag_rows(adj_ref):
    line = lax.broadcasted_iota(jnp.int32, (STAT, BLOCK), 0)
    stat = jnp.zeros((STAT, BLOCK), F32)
    for i in range(2 * WINDOW):
        flag = (adj_ref[0, i // WINDOW, 0, i % WINDOW] == 1).astype(jnp.int32).astype(F32)
        stat = jnp.where(line == 8 + i, flag, stat)
    return line, stat


def pack_head(line, stat, diagonal, g, o, lse_row):
    delta_row = jnp.sum(jnp.where(diagonal, contract(o, g, 1, 1), 0.0), axis=0, keepdims=True)
    for i, row in enumerate(list(three_pieces(lse_row)) + list(three_pieces(delta_row))):
        stat = jnp.where(line == i, jnp.broadcast_to(row, (STAT, BLOCK)), stat)
    return stat.astype(BF16)


def contract(a, b, da, db):
    return lax.dot_general(a, b, (((da,), (db,)), ((), ())), preferred_element_type=F32)


def unpack_stat(stat, row, slot_flag):
    stat = stat.astype(F32)
    lse = stat[0:1] + stat[1:2] + stat[2:3]
    delta = stat[3:4] + stat[4:5] + stat[5:6]
    keep = slot_flag(stat, 8 + WINDOW * row) > 0.5
    return jnp.where(keep, lse * LOG2E, FAR_AWAY), delta


def flag_of(w):
    return lambda stat, base: stat[base + w:base + w + 1]


def flag_by_parity(odd, w_even, w_odd):
    return lambda stat, base: jnp.where(
        odd == 1, stat[base + w_odd:base + w_odd + 1], stat[base + w_even:base + w_even + 1])


def terms(q, g, k, v, lse, delta):
    scores = contract(k, q, 1, 1) * (SCALE * LOG2E)
    prob = jnp.exp2(scores - lse)
    grad = prob * (contract(v, g, 1, 1) - delta)
    low = prob.astype(BF16)
    grad = grad.astype(BF16)
    dv = contract(low, g, 1, 0)
    dk = contract(grad, q, 1, 0) * SCALE
    dq = contract(grad, k, 0, 0) * SCALE
    return dq, dk, dv

def vmem(shape, dtype):
    return pltpu.VMEM(shape, dtype)


def on_chip(value):
    return pltpu.with_memory_space_constraint(value, pltpu.VMEM)


def call_on_chip(kernel, name, odd, inputs, outs, flops, exps=0, after=None):
    spec = pl.BlockSpec(memory_space=pltpu.VMEM)
    moved_bytes = sum(x.size * x.dtype.itemsize for x in inputs)
    return pl.pallas_call(
        kernel,
        in_specs=[pl.BlockSpec(memory_space=pltpu.SMEM)] + [spec] * len(inputs),
        out_specs=[spec] * len(outs),
        out_shape=[vmem(s, t) for s, t in outs],
        compiler_params=pltpu.CompilerParams(vmem_limit_bytes=16 * 2**20),
        cost_estimate=pl.CostEstimate(flops=flops, bytes_accessed=moved_bytes, transcendentals=exps),
        name=name,
    )(odd, *[on_chip(x) for x in inputs])


def arrived_kernel(*refs):
    refs[-1][...] = jnp.zeros((8, HEAD_DIM), F32)


def arrived(*inputs):
    spec = pl.BlockSpec(memory_space=pltpu.VMEM)
    return pl.pallas_call(
        arrived_kernel,
        in_specs=[spec] * len(inputs),
        out_specs=spec,
        out_shape=vmem((8, HEAD_DIM), F32),
        compiler_params=pltpu.CompilerParams(vmem_limit_bytes=2**20),
        cost_estimate=pl.CostEstimate(flops=WAIT_FLOPS, bytes_accessed=2**20, transcendentals=0),
        name="arrived",
    )(*[on_chip(x) for x in inputs])


WAIT_FLOPS = 10**11
PACK_STEP = 4


def pack_kernel(odd_ref, adj_hbm, lse_hbm, q_hbm, k_hbm, v_hbm, o_hbm, g_hbm,
                xqa, xka, xqb, xkb, cross, q_in, k_in, v_in, o_in, g_in, lse_ref, adj_ref, sems, lse_sem, adj_sem):
    adj_copy = pltpu.make_async_copy(adj_hbm, adj_ref, adj_sem)
    adj_copy.start()
    lse_copy = pltpu.make_async_copy(lse_hbm, lse_ref, lse_sem)
    lse_copy.start()
    width = PACK_STEP * HEAD_DIM
    chunks = 2 * HALF // PACK_STEP
    copies = []
    for c in range(chunks):
        cols = pl.ds(c * width, width)
        copies.append([
            pltpu.make_async_copy(a.at[:, cols], b.at[:, cols], sems.at[c, i])
            for i, (a, b) in enumerate(
                [(q_hbm, q_in), (g_hbm, g_in), (o_hbm, o_in), (k_hbm, k_in), (v_hbm, v_in)])])
        for copy in copies[c]:
            copy.start()
    adj_copy.wait()
    lse_copy.wait()
    line, stat = flag_rows(adj_ref)
    diagonal = (lax.broadcasted_iota(jnp.int32, (BLOCK, BLOCK), 0)
                == lax.broadcasted_iota(jnp.int32, (BLOCK, BLOCK), 1))
    for c in range(chunks):
        for copy in copies[c]:
            copy.wait()
        for head in range(c * PACK_STEP, (c + 1) * PACK_STEP):
            cols = slice(head * HEAD_DIM, (head + 1) * HEAD_DIM)
            h = head % HALF
            xq, xk = (xqa, xka) if head < HALF else (xqb, xkb)
            xq[h, 0:128, :] = q_in[:, cols]
            xq[h, 128:256, :] = g_in[:, cols]
            xq[h, 256:272, :] = pack_head(
                line, stat, diagonal, g_in[:, cols], o_in[:, cols], lse_ref[head:head + 1])
            xk[h, 0:128, :] = k_in[:, cols]
            xk[h, 128:256, :] = v_in[:, cols]
            if head >= HALF:
                xk[h, KROWS:QROWS, :] = jnp.zeros((STAT, HEAD_DIM), BF16)

    is_odd = odd_ref[0] == 1

    @pl.when(is_odd)
    def _():
        cross[...] = xqa[...]

    @pl.when(jnp.logical_not(is_odd))
    def _():
        cross[...] = xkb[...]


def pack(odd, adjacency, queries, keys, values, outputs, d_out, row_lse):
    smem = pl.BlockSpec(memory_space=pltpu.SMEM)
    spec = pl.BlockSpec(memory_space=pltpu.VMEM)
    anywhere = pl.BlockSpec(memory_space=pltpu.HBM)
    shapes = [QROWS, KROWS, QROWS, QROWS, QROWS]
    return pl.pallas_call(
        pack_kernel,
        in_specs=[smem] + [anywhere] * 7,
        out_specs=[spec] * len(shapes),
        out_shape=[vmem((HALF, s, HEAD_DIM), BF16) for s in shapes],
        scratch_shapes=[pltpu.VMEM((BLOCK, 2 * HALF * HEAD_DIM), BF16)] * 5
        + [pltpu.VMEM((2 * HALF, BLOCK), F32), pltpu.SMEM((1, 2, 1, WINDOW), jnp.int32),
           pltpu.SemaphoreType.DMA((2 * HALF // PACK_STEP, 5)), pltpu.SemaphoreType.DMA, pltpu.SemaphoreType.DMA],
        compiler_params=pltpu.CompilerParams(vmem_limit_bytes=16 * 2**20),
        cost_estimate=pl.CostEstimate(flops=10**8, bytes_accessed=5 * 2**20, transcendentals=0),
        name="pack",
    )(odd, *[pltpu.with_memory_space_constraint(x, pltpu.HBM)
             for x in (adjacency, row_lse, queries, keys, values, outputs, d_out)])


Q3 = slice(0, QROWS)
K3 = slice(QROWS, QROWS + KROWS)
NEAR_Q = slice(QROWS + KROWS, 2 * QROWS + KROWS)
NEAR_K = slice(QROWS + KROWS, QROWS + 2 * KROWS)
MATE_ROWS = 2 * QROWS + KROWS


def mates_kernel(odd_ref, xqa, xkb, q2, k2, out):
    def one_head(h, carry):
        out[h, Q3] = q2[h]
        out[h, K3] = k2[h, 0:KROWS]
        return carry

    lax.fori_loop(0, HALF, one_head, 0)
    is_odd = odd_ref[0] == 1

    @pl.when(is_odd)
    def _():
        out[:, NEAR_Q, :] = xkb[...]

    @pl.when(jnp.logical_not(is_odd))
    def _():
        out[:, NEAR_Q, :] = xqa[...]


def attend_a_kernel(odd_ref, here, xqa, cross, q2, mates, xka, fk,
                    q_own, q_two, kv_own, swap_out, down_out, far_out):
    odd = odd_ref[0]
    is_odd = odd == 1
    flags = [flag_of(0), flag_by_parity(odd, 3, 1), flag_of(2), flag_by_parity(odd, 1, 3)]

    def one_head(h, carry):
        slots = [xqa[h], jnp.where(is_odd, mates[h, NEAR_Q], cross[h]), q2[h], mates[h, Q3]]
        q = jnp.concatenate([s[0:128] for s in slots], axis=0)
        g = jnp.concatenate([s[128:256] for s in slots], axis=0)
        lse = []
        for row in range(2):
            both = [unpack_stat(s[256:272], row, f) for s, f in zip(slots, flags)]
            lse.append(jnp.broadcast_to(jnp.concatenate([b[0] for b in both], axis=1), (128, 512)))
            delta = jnp.concatenate([b[1] for b in both], axis=1)
        k = jnp.concatenate([xka[h, 0:128], fk[h, 0:128]], axis=0)
        v = jnp.concatenate([xka[h, 128:256], fk[h, 128:256]], axis=0)
        dq, dk, dv = terms(q, g, k, v, jnp.concatenate(lse, axis=0), delta)
        q_own[h] = dq[0:128]
        down_out[h] = dq[128:256].astype(BF16)
        q_two[h] = dq[256:384]
        swap_out[h] = dq[384:512].astype(BF16)
        kv_own[h, 0:128] = dk[0:128]
        kv_own[h, 128:256] = dv[0:128]
        far_out[h, 0:128] = dk[128:256].astype(BF16)
        far_out[h, 128:256] = dv[128:256].astype(BF16)
        return carry

    lax.fori_loop(0, HALF, one_head, 0, unroll=4)


def attend_b_kernel(odd_ref, here, xkb, cross, k2, mates, xqb, fq,
                    kv_own, kv_two, q_own, swap_out, up_out, far_out):
    odd = odd_ref[0]
    is_odd = odd == 1
    flags = [flag_of(0), flag_by_parity(odd, 1, 3), flag_of(2), flag_by_parity(odd, 3, 1)]

    def one_head(h, carry):
        slots = [xkb[h], jnp.where(is_odd, cross[h, 0:KROWS], mates[h, NEAR_K]), k2[h], mates[h, K3]]
        k = jnp.concatenate([s[0:128] for s in slots], axis=0)
        v = jnp.concatenate([s[128:256] for s in slots], axis=0)
        q = jnp.concatenate([xqb[h, 0:128], fq[h, 0:128]], axis=0)
        g = jnp.concatenate([xqb[h, 128:256], fq[h, 128:256]], axis=0)
        stat_own, stat_far = xqb[h, 256:272], fq[h, 256:272]
        lse = []
        for f in flags:
            own, own_delta = unpack_stat(stat_own, 0, f)
            far, far_delta = unpack_stat(stat_far, 1, f)
            lse.append(jnp.broadcast_to(jnp.concatenate([own, far], axis=1), (128, 256)))
            delta = jnp.concatenate([own_delta, far_delta], axis=1)
        dq, dk, dv = terms(q, g, k, v, jnp.concatenate(lse, axis=0), delta)
        q_own[h] = dq[0:128]
        far_out[h] = dq[128:256].astype(BF16)
        kv_own[h, 0:128] = dk[0:128]
        kv_own[h, 128:256] = dv[0:128]
        up_out[h, 0:128] = dk[128:256].astype(BF16)
        up_out[h, 128:256] = dv[128:256].astype(BF16)
        kv_two[h, 0:128] = dk[256:384]
        kv_two[h, 128:256] = dv[256:384]
        swap_out[h, 0:128] = dk[384:512].astype(BF16)
        swap_out[h, 128:256] = dv[384:512].astype(BF16)
        return carry

    lax.fori_loop(0, HALF, one_head, 0, unroll=4)


def block(rows, dtype):
    return ((HALF, rows, HEAD_DIM), dtype)


def attend_a(odd, *inputs):
    outs = [block(128, F32), block(128, F32), block(256, F32), block(128, BF16), block(128, BF16), block(256, BF16)]
    return call_on_chip(attend_a_kernel, "attend_a", odd, inputs, outs, 13 * 10**8, 2**20)


def attend_b(odd, *inputs):
    outs = [block(256, F32), block(256, F32), block(128, F32), block(256, BF16), block(256, BF16), block(128, BF16)]
    return call_on_chip(attend_b_kernel, "attend_b", odd, inputs, outs, 13 * 10**8, 2**20)


def combine_kernel(odd_ref, mine, swapped, total):
    def one_head(h, carry):
        total[h] = (mine[h] + swapped[h].astype(F32)).astype(BF16)
        return carry

    lax.fori_loop(0, HALF, one_head, 0)


def combine(name, odd, *inputs):
    return call_on_chip(combine_kernel, name, odd, inputs, [(inputs[0].shape, BF16)], 10**6)[0]


def finish_kernel(first, grads, outs, stage, sems):
    copies = []
    step = 2
    for h in range(HALF):
        cols = slice(h * HEAD_DIM, (h + 1) * HEAD_DIM)
        for part, grad in zip(stage, grads(h)):
            part[:, cols] = grad.astype(BF16)
        if h % step == step - 1:
            c = h // step
            width = step * HEAD_DIM
            for i, (part, out) in enumerate(zip(stage, outs)):
                copies.append(pltpu.make_async_copy(
                    part.at[:, pl.ds(c * width, width)],
                    out.at[:, pl.ds(first * HEAD_DIM + c * width, width)], sems.at[c, i]))
                copies[-1].start()
    for copy in copies:
        copy.wait()


def finish_b_kernel(k_own, q_b, up, up_sum, far_q, dq, dk, dv, *scratch):
    def grads(h):
        kv = k_own[h] + up_sum[h].astype(F32) + up[h].astype(F32)
        return q_b[h] + far_q[h].astype(F32), kv[0:128], kv[128:256]

    finish_kernel(HALF, grads, (dq, dk, dv), scratch[0:3], scratch[3])


def finish_a_kernel(q_own, kv_a, down, down_sum, far_k, dq_in, dk_in, dv_in, dq, dk, dv, *scratch):
    def grads(h):
        kv = kv_a[h] + far_k[h].astype(F32)
        return q_own[h] + down_sum[h].astype(F32) + down[h].astype(F32), kv[0:128], kv[128:256]

    finish_kernel(0, grads, (dq, dk, dv), scratch[0:3], scratch[3])


def finish(kernel, name, flops, inputs, partial=()):
    spec = pl.BlockSpec(memory_space=pltpu.VMEM)
    anywhere = pl.BlockSpec(memory_space=pltpu.HBM)
    whole = jax.ShapeDtypeStruct((BLOCK, 2 * HALF * HEAD_DIM), BF16)
    return pl.pallas_call(
        kernel,
        in_specs=[spec] * len(inputs) + [anywhere] * len(partial),
        out_specs=[anywhere] * 3,
        out_shape=[whole] * 3,
        input_output_aliases={len(inputs) + i: i for i in range(len(partial))},
        scratch_shapes=[pltpu.VMEM((BLOCK, HALF * HEAD_DIM), BF16)] * 3 + [pltpu.SemaphoreType.DMA((HALF // 2, 3))],
        compiler_params=pltpu.CompilerParams(vmem_limit_bytes=8 * 2**20),
        cost_estimate=pl.CostEstimate(flops=flops, bytes_accessed=3 * 2**20, transcendentals=0),
        name=name,
    )(*[on_chip(x) for x in inputs], *partial)


def moved(value, axis, steps):
    count = lax.axis_size(axis)
    return lax.ppermute(value, axis, [(i, (i + steps) % count) for i in range(count)])


def exchanged(value):
    count = lax.axis_size("ka")
    return lax.ppermute(value, "ka", [(i, i ^ 1) for i in range(count)])


def crossed(value, odd_steps, even_steps):
    count = lax.axis_size("ka")
    return lax.ppermute(
        value, "ka", [(i, (i + (odd_steps if i % 2 == 1 else even_steps)) % count) for i in range(count)])


def local(queries, keys, values, outputs, d_out, row_lse, adjacency):
    odd = (lax.axis_index("ka") % 2).astype(jnp.int32).reshape(1)
    xqa, xka, xqb, xkb, cross = pack(
        odd, adjacency.transpose(0, 1, 3, 2), queries, keys, values, outputs, d_out, row_lse)
    fq = moved(xqb, "pb", 1)
    q2 = moved(xqa, "ka", 2)
    k2 = moved(xkb, "ka", -2)
    cross = crossed(cross, 3, -3)
    mates = call_on_chip(mates_kernel, "mates", odd, (xqa, xkb, q2, k2), [block(MATE_ROWS, BF16)], 10**5)[0]
    mates, xka = lax.optimization_barrier((mates, xka))
    mates = exchanged(mates)
    fk = moved(xka, "pb", -1)
    here = arrived(fq, cross)
    k_own, k_two, q_b, swap_b, up, far_q = attend_b(odd, here, xkb, cross, k2, mates, xqb, fq)
    far_q = moved(far_q, "pb", -1)
    swap_b, fk = lax.optimization_barrier((exchanged(swap_b), fk))
    b_sum = combine("combine_b", odd, k_two, swap_b)
    xka, b_sum, up = lax.optimization_barrier((xka, b_sum, up))
    up = crossed(up, 3, 1)
    up_sum = moved(b_sum, "ka", 2)
    q_own, q_two, kv_a, swap_a, down, far_k = attend_a(odd, here, xqa, cross, q2, mates, xka, fk)
    down, swap_a, far_k, far_q = lax.optimization_barrier((down, swap_a, far_k, far_q))
    down = crossed(down, -1, -3)
    far_k = moved(far_k, "pb", 1)
    down_sum = moved(combine("combine_a", odd, q_two, exchanged(swap_a)), "ka", -2)
    grads = finish(finish_b_kernel, "finish_b", WAIT_FLOPS, (k_own, q_b, up, up_sum, far_q))
    return tuple(finish(finish_a_kernel, "finish_a", 10**6, (q_own, kv_a, down, down_sum, far_k), grads))


def solution(mesh):
    rows = P(("pb", "ka"), None)
    placed = (rows, rows, rows, rows, rows, P(None, ("pb", "ka")), P(("pb", "ka"), None, None, None))
    return jax.shard_map(
        local,
        mesh=mesh,
        in_specs=placed,
        out_specs=(rows, rows, rows),
        check_vma=False,
    )
```
